32 devices in a mesh: tm: 16 (over z, y, x), cells: 2 (over core).
Axes of the slice: x: 2, y: 2, z: 4, core: 2. Of those that a mesh axis runs over, the one named last changes fastest.
Arguments:
- flux: bfloat16 [64, 128, 8192], P(None, 'tm', 'cells'), may hold values from -6 to 6
- footprint: bfloat16 [4096, 4, 8192], P('tm', None, 'cells'), may hold values from -0.046875 to 0.046875
- band_lag: int32 [4096, 4], P('tm'), may hold values from 0 to 23, as said below
- obs_hour: int32 [4096], P('tm'), may hold values from 0 to 127, as said below
- tile_mask: int32 [4096, 64], P('tm', 'cells'), may hold values 0 or 1
- obs_value: float32 [64, 4096], P(None, 'tm'), may hold values from -6 to 6
- obs_weight: float32 [4096], P('tm'), may hold values from 4 to 64
Outputs:
- modeled: float32 [64, 4096], P(None, 'tm')
- gradient: float32 [64, 128, 8192], P(None, 'tm', 'cells')
The draws below stay inside these ranges and needn't reach their ends.
Inputs may be any that keep to these rules, and one draw needn't show every extreme that they name: `band_lag`: each row holds 4 different lags. `obs_hour`: observation i has an hour in [(i // 256) * 8, (i // 256 + 1) * 8).
All inputs are finite; a program needn't handle non-finite values. No bound on the sum of `tile_mask` on one device may be relied on, other than what follows from the above.
Results may differ from the reference program's by a relative error of at most 0.0029.
Values may be sent and summed in bfloat16 or wider, within the bound.
A program may use at most 320 MiB of HBM per device.

```python
import math
import jax
import jax.numpy as jnp
from jax import lax

LAGS = 24
BANDS = 4
HOURS_DEV = 8
TILE = 128
OBS_DEV = 256
SAMPLES = 64
HOURS = 128
OBS = 4096
CELLS = 8192
TILES = 64


def draw_band_lag(key, part):
    scores = jax.random.randint(jax.random.fold_in(key, 11), (OBS, LAGS), 0, 1048576)
    scores = scores * LAGS + jnp.arange(LAGS, dtype=jnp.int32)[None, :]
    ordering = jnp.argsort(scores, axis=1, stable=True)
    return ordering[:, :BANDS].astype(jnp.int32)


def draw_obs_hour(key, part):
    owner = jnp.arange(OBS, dtype=jnp.int32) // OBS_DEV
    within = jax.random.randint(jax.random.fold_in(key, 23), (OBS,), 0, HOURS_DEV)
    return (owner * HOURS_DEV + within).astype(jnp.int32)


def with_ends(entries, rng, least, top_value):
    longest = entries.shape.index(max(entries.shape))
    spots = []
    for shift in (0, 1):
        where = [jax.random.randint(jax.random.fold_in(rng, axis), (), 0, length) for axis, length in enumerate(entries.shape)]
        where[longest] = (where[longest] + shift) % entries.shape[longest]
        spots.append(tuple(where))
    return entries.at[spots[0]].set(least).at[spots[1]].set(top_value)


def block_levels(rng, shape, cuts, low, top_value):
    level, own = 1.0, jax.random.fold_in(rng, 6)
    for position, blocks in cuts:
        heights = jnp.exp(jax.random.uniform(jax.random.fold_in(own, position), (blocks,), jnp.float32, low / len(cuts), top_value / len(cuts)))
        level = level * jnp.repeat(heights, shape[position] // blocks).reshape([-1 if axis == position else 1 for axis in range(len(shape))])
    return level


def scatter_about(stream_key, extent, deviation, most, cuts=(), kind=jnp.bfloat16):
    result = jax.random.normal(stream_key, extent, jnp.float32) * deviation
    if len(cuts) > 0:
        result = block_levels(stream_key, extent, cuts, -0.22, 0.18) * result
    return jnp.clip(result, min=-most, max=most).astype(kind)


def setup_inputs(seed: int = 0) -> dict:
    key_list = jax.random.split(jax.random.key(seed), 8)
    flux = scatter_about(key_list[0], (SAMPLES, HOURS, CELLS), 1.0, 6.0, ((1, 16), (2, 2)))
    footprint = scatter_about(key_list[1], (OBS, BANDS, CELLS), (BANDS * CELLS // 2) ** -0.5, 0.046875, ((0, 16), (2, 2)))
    band_lag = draw_band_lag(jax.random.fold_in(key_list[7], 71), 0)
    obs_hour = draw_obs_hour(jax.random.fold_in(key_list[7], 71), 0)
    tile_mask = with_ends((jax.random.randint(key_list[4], (OBS, TILES), 0, 2) < 1).astype(jnp.int32), jax.random.fold_in(key_list[4], 1), 0, 1)
    obs_value = scatter_about(key_list[5], (SAMPLES, OBS), 1.0, 6.0, ((1, 16),), jnp.float32)
    obs_weight = jnp.clip(jnp.exp(math.log(64.0) - 2.7725887 * jax.random.uniform(key_list[6], (OBS,), jnp.float32) ** block_levels(key_list[6], (OBS,), ((0, 16),), -0.2, 0.2)), 4.0, 64.0)
    return {"flux": flux, "footprint": footprint, "band_lag": band_lag, "obs_hour": obs_hour, "tile_mask": tile_mask, "obs_value": obs_value, "obs_weight": obs_weight}


def reference(flux, footprint, band_lag, obs_hour, tile_mask, obs_value, obs_weight):
    group_rows = 8
    groups = OBS // group_rows
    source = obs_hour[:, None] - band_lag
    in_range = (source >= 0).astype(jnp.float32)
    hour_index = jnp.maximum(source, 0).astype(jnp.int32)

    def weights_of(prints, tiles_on, inside):
        spread = jnp.repeat(tiles_on.astype(jnp.float32), TILE, axis=1)
        return prints.astype(jnp.float32) * spread[:, None, :] * inside[:, :, None]

    grouped = (footprint.reshape(groups, group_rows, BANDS, CELLS),
               tile_mask.reshape(groups, group_rows, TILES),
               in_range.reshape(groups, group_rows, BANDS),
               hour_index.reshape(groups, group_rows, BANDS))

    def forward(inputs):
        prints, tiles_on, inside, hours_at = inputs
        weighted = weights_of(prints, tiles_on, inside)
        picked = jnp.take(flux, hours_at.reshape(-1), axis=1).astype(jnp.float32)
        picked = picked.reshape(SAMPLES, group_rows, BANDS, CELLS)
        return jnp.einsum('sobc,obc->so', picked, weighted, precision=lax.Precision.HIGHEST)

    modeled = lax.map(forward, grouped)
    modeled = jnp.transpose(modeled, (1, 0, 2)).reshape(SAMPLES, OBS)
    residual = (obs_weight[None, :] * (modeled - obs_value)).astype(jnp.bfloat16)
    misfit = jnp.transpose(residual.astype(jnp.float32).reshape(SAMPLES, groups, group_rows), (1, 0, 2))

    def adjoint(accumulated, inputs):
        prints, tiles_on, inside, hours_at, weighted_res = inputs
        weighted = weights_of(prints, tiles_on, inside)
        contrib = jnp.einsum('so,obc->sobc', weighted_res, weighted, precision=lax.Precision.HIGHEST)
        contrib = contrib.reshape(SAMPLES, group_rows * BANDS, CELLS)
        accumulated = accumulated.at[:, hours_at.reshape(-1), :].add(contrib)
        return accumulated, None

    gradient, _ = lax.scan(adjoint, jnp.zeros((SAMPLES, HOURS, CELLS), jnp.float32), grouped + (misfit,))
    return modeled, gradient
```

```python
import functools
import math

import jax
import jax.numpy as jnp
from jax import lax
from jax.experimental import pallas as pl
from jax.experimental.pallas import tpu as pltpu
from jax.sharding import PartitionSpec as P

LAGS = 24
GRAIN = 16
GROUP = 2
TILE_CELLS = 512
VMEM_LIMIT = 62 * 2**20
MESH = pl.DeviceIdType.MESH
BF16 = jnp.bfloat16
F32 = jnp.float32


def shifted(value, axis, steps):
    count = lax.axis_size(axis)
    initial, last = (max(0, -steps), min(count, count - steps))
    return lax.ppermute(value, axis, [(source, source + steps) for source in range(initial, last)])


def over_axis(value, axis):
    if lax.axis_size(axis) == 2:
        return value + lax.ppermute(value, axis, [(0, 1), (1, 0)])
    return lax.psum(value, axis)


def contract(left, right, left_dim, right_dim, out=F32, precision=None):
    return lax.dot_general(
        left, right, (((left_dim,), (right_dim,)), ((), ())),
        precision=precision, preferred_element_type=out,
    )


def capacities(block, hours, obs, bands):
    mean = spread = mean_square = 0.0
    for hour in range(hours):
        hits = sum(1 for lag in range(LAGS) if (hour - lag) // hours == -block)
        share = hits / LAGS
        mean += bands * share / hours
        mean_square += (bands * share) ** 2 / hours
        spread += bands * share * (1 - share) * (LAGS - bands) / (LAGS - 1) / hours
    spread += mean_square - mean**2
    rows = obs * mean + 4.0 * math.sqrt(obs * spread)
    half_spread = 0.5 * (spread + mean**2) - 0.25 * mean**2
    slots = 0.5 * obs * mean + 4.7 * math.sqrt(obs * half_spread)
    rows = min(obs * bands, GRAIN * math.ceil(rows / GRAIN))
    return rows, min(rows, GRAIN * math.ceil(slots / GRAIN))


def prep_kernel(caps, slots, lag_ref, hour_ref, mask_ref, band_ref, pos_ref, flag_ref, *meta_refs):
    reach = len(caps) - 1
    bands, obs = lag_ref.shape
    tiles = mask_ref.shape[0]
    rows = bands * obs
    hours = meta_refs[0].shape[0] - tiles - 8
    position = lax.axis_index("tm")
    first = (position - reach) * hours
    row_ids = lax.broadcasted_iota(jnp.int32, (obs, rows), 1)
    obs_ids = lax.broadcasted_iota(jnp.int32, (obs, rows), 0)
    spread = ((row_ids >= obs_ids * bands) & (row_ids < (obs_ids + 1) * bands)).astype(F32).astype(BF16)
    ahead = hour_ref[...] - lag_ref[...] - first
    ahead = jnp.concatenate([ahead, jnp.zeros((8 - bands % 8, obs), jnp.int32)], axis=0) if bands % 8 else ahead
    ahead = jnp.dot(ahead.astype(F32).astype(BF16), spread, preferred_element_type=F32)
    ahead = jnp.sum(ahead * band_ref[...], axis=0, keepdims=True)
    on = jnp.dot(mask_ref[...].astype(F32).astype(BF16), spread, preferred_element_type=F32)
    ids = lax.broadcasted_iota(jnp.int32, (8, obs), 1).astype(F32) + 1.0
    ids = jnp.dot(ids.astype(BF16), spread, preferred_element_type=F32)[:1]
    valid = ahead >= (-first).astype(F32)
    members, lines = [], []
    for block in range(reach + 1):
        low = hours * (reach - block)
        member = (ahead >= low) & (ahead < low + hours) & valid
        members.append(member.astype(F32))
    head = jnp.concatenate(members + [jnp.zeros((8 - (reach + 1) % 8, rows), F32)], axis=0)
    lines = [head] + [members[block] * on for block in range(1, reach + 1)]
    before = lax.broadcasted_iota(jnp.int32, (rows, rows), 0) < lax.broadcasted_iota(jnp.int32, (rows, rows), 1)
    before = before.astype(F32).astype(BF16)
    ranks = jnp.dot(jnp.concatenate(lines, axis=0).astype(BF16), before, preferred_element_type=F32)
    over = jnp.zeros((1, rows), F32)
    pos = jnp.full((tiles, rows), -1.0, F32)
    base = caps[0]
    for block in range(reach + 1):
        member = members[block]
        rank = ranks[block : block + 1]
        over = jnp.maximum(over, jnp.where((member > 0) & (rank >= caps[block]), 1.0, 0.0))
        row_slot = jnp.where(member > 0, rank, -1.0)
        if block == 0:
            pos = jnp.where((member * on > 0) & (rank < caps[0]), rank, pos)
            order = jnp.zeros((tiles, rows), F32)
        else:
            start = head.shape[0] + (block - 1) * tiles
            tile_rank = ranks[start : start + tiles]
            inside = member * on > 0
            excess = jnp.where(inside & (tile_rank >= slots[block]), 1.0, 0.0)
            over = jnp.maximum(over, jnp.max(excess, axis=0, keepdims=True))
            pos = jnp.where(inside & (tile_rank < slots[block]), tile_rank + base, pos)
            order = jnp.where(inside, tile_rank + 1.0, 0.0)
            base += slots[block]
        hour_of = lax.broadcasted_iota(jnp.int32, (hours, rows), 0).astype(F32) + float(hours * (reach - block))
        match = jnp.where((ahead == hour_of) & valid, 1.0, 0.0)
        tail = jnp.where(lax.broadcasted_iota(jnp.int32, (8, rows), 0) == 0, ids, 0.0)
        values = jnp.concatenate([order, match, tail], axis=0).astype(BF16)
        select = lax.broadcasted_iota(jnp.int32, (caps[block], rows), 0).astype(F32) == row_slot
        select = select.astype(F32).astype(BF16)
        meta_refs[block][...] = contract(values, select, 1, 1).astype(BF16)
    pos_ref[...] = pos
    flag_ref[...] = jnp.broadcast_to(jnp.max(over, axis=1, keepdims=True), (8, 128))


def prepare(caps, slots, hours, band_lag, obs_hour, tile_mask):
    obs, bands = band_lag.shape
    tiles = tile_mask.shape[1]
    rows = obs * bands
    pad = bands + (8 - bands % 8 if bands % 8 else 0)
    band = (jnp.arange(rows) % bands == jnp.arange(pad)[:, None]).astype(F32)
    vmem = pl.BlockSpec(memory_space=pltpu.VMEM)
    shapes = [
        jax.ShapeDtypeStruct((tiles, rows), F32),
        jax.ShapeDtypeStruct((8, 128), F32),
    ] + [jax.ShapeDtypeStruct((tiles + hours + 8, cap), BF16) for cap in caps]
    return pl.pallas_call(
        functools.partial(prep_kernel, caps, slots),
        in_specs=[vmem] * 4,
        out_specs=[vmem] * len(shapes),
        out_shape=shapes,
        compiler_params=pltpu.CompilerParams(vmem_limit_bytes=VMEM_LIMIT),
        name="prep",
    )(band_lag.T, obs_hour[None, :], tile_mask.T, band)


def split_dot(left, right, left_dim, right_dim):
    total = None
    for _ in range(3):
        term = left.astype(BF16)
        left = left - term.astype(F32)
        part = contract(term, right, left_dim, right_dim)
        total = part if total is None else total + part
    return total


def bulk_kernel(geometry, *refs):
    caps, slots, tiles, hours, axis = geometry
    reach = len(caps) - 1
    blocks = range(1, reach + 1)
    refs = list(refs)

    def take(count):
        head = refs[:count]
        del refs[:count]
        return head

    (prints_ref, flux_hbm, pos_ref, flag_ref, value_ref, weight_ref) = take(6)
    meta_refs = take(reach + 1)
    (dense_ref, modeled_ref, flag_out) = take(3)
    line_refs = take(reach + 1)
    match_refs = take(reach)
    (prints_buf, flux_ref, local_buf, dense_buf, part_own, part_in, total_buf, other_buf,
     res_buf, res_in, flag_buf, flag_in) = take(12)
    send_refs, recv_refs, found_refs, got_refs, column_refs = (
        take(reach), take(reach), take(reach + 1), take(reach), take(reach))
    (relay_ref, relay_one) = take(2)
    (prints_sem, flux_sem, local_sem, dense_sem, send_sem, recv_sem, relay_in_sem, relay_out_sem,
     one_in_sem, one_out_sem, meta_send, meta_recv, part_send, part_recv, core_sem, res_send, res_recv,
     flag_sem) = take(18)

    me = lax.axis_index("tm")
    core = lax.axis_index("cells")
    obs = value_ref.shape[1]
    samples = value_ref.shape[0]
    groups = tiles // GROUP
    wide = GROUP * 128
    quad = lax.rem(me, 4)
    relays = axis % 4 == 0 and reach >= 2

    def to(tm):
        return {"tm": tm}

    partners = [step for step in (1, 2, 3, 4) if step < axis]
    hops = []
    step = 1
    while step < axis:
        hops.append(step)
        step *= 2
    far = [hop for hop in hops if hop > 4]

    def flip(hop):
        return jnp.where(lax.rem(me // hop, 2) == 0, me + hop, me - hop)

    barrier = pltpu.get_barrier_semaphore()
    count = jnp.int32(0)
    for step in partners:
        for target, exists in ((me + step, me + step < axis), (me - step, me >= step)):
            @pl.when(exists)
            def _():
                pl.semaphore_signal(barrier, inc=1, device_id=to(target), device_id_type=MESH)
            count = count + exists.astype(jnp.int32)
    for hop in far:
        pl.semaphore_signal(barrier, inc=1, device_id=to(flip(hop)), device_id_type=MESH)
        count = count + 1
    pl.semaphore_signal(barrier, inc=1, device_id={"cells": 1 - core}, device_id_type=MESH)
    count = count + 1

    def fetch(group, slot):
        return pltpu.make_async_copy(
            prints_ref.at[:, :, pl.ds(pl.multiple_of(group * wide, wide), wide)],
            prints_buf.at[slot], prints_sem.at[slot])

    fetch(0, 0).start()
    flux_copy = pltpu.make_async_copy(flux_hbm, flux_ref, flux_sem)
    flux_copy.start()
    pl.semaphore_wait(barrier, count)

    def remote(src, dst, ssem, rsem, target):
        return pltpu.make_async_remote_copy(
            src_ref=src, dst_ref=dst, send_sem=ssem, recv_sem=rsem,
            device_id=target, device_id_type=MESH)

    def meta_copy(block, target):
        return remote(meta_refs[block], got_refs[block - 1], meta_send.at[block - 1], meta_recv.at[block - 1], to(target))

    for block in blocks:
        @pl.when(me >= block)
        def _():
            meta_copy(block, me - block).start()

    def part_of(group):
        return pl.ds(group * GROUP, GROUP)

    def bulk_copy(block, group, source, target, dst=None, ssem=None, rsem=None):
        return remote(source, recv_refs[block - 1].at[part_of(group)] if dst is None else dst,
                      send_sem.at[block - 1, group] if ssem is None else ssem,
                      recv_sem.at[block - 1, group] if rsem is None else rsem, to(target))

    def sends(group, blocks_now, act):
        for block in blocks_now:
            source = send_refs[block - 1].at[part_of(group)]
            exists = me >= block
            detour = None
            if relays and block == 2:
                detour = quad == 0
                copy = bulk_copy(2, group, source, me + 2, relay_ref.at[part_of(group)], None, relay_in_sem.at[group])
            elif relays and block == 1:
                detour = (lax.rem(me, 2) == 0) & (lax.rem(group, 4) == 3)
                copy = bulk_copy(1, group, source, jnp.where(quad == 0, me + 2, me - 2),
                                 relay_one.at[part_of(group // 4)], None, one_in_sem.at[group // 4])
            if detour is None:
                @pl.when(exists)
                def _():
                    act(bulk_copy(block, group, source, me - block))
            else:
                @pl.when(exists & detour)
                def _():
                    act(copy)

                @pl.when(exists & jnp.logical_not(detour))
                def _():
                    act(bulk_copy(block, group, source, me - block))

    def forward_two(group):
        return bulk_copy(2, group, relay_ref.at[part_of(group)], me - 4, None, relay_out_sem.at[group])

    def forward_one(group):
        return bulk_copy(1, group, relay_one.at[part_of(group // 4)], jnp.where(quad == 0, me + 1, me - 3),
                         None, one_out_sem.at[group // 4])

    is_two = (quad == 2) & (me >= 6)
    is_one = (lax.rem(me, 2) == 0) & (me != 2)
    late = [3] if relays and reach >= 3 else []
    early = [block for block in blocks if block not in late]

    def relay(group):
        if late:
            @pl.when(quad == 2)
            def _():
                sends(group, late, lambda copy: copy.start())
        if relays:
            @pl.when(is_two)
            def _():
                bulk_copy(2, group, send_refs[1].at[part_of(group)], me - 4, relay_ref.at[part_of(group)],
                          None, relay_in_sem.at[group]).wait_recv()
                forward_two(group).start()

            @pl.when(is_one & (lax.rem(group, 4) == 3))
            def _():
                bulk_copy(1, group, send_refs[0].at[part_of(group)], me, relay_one.at[part_of(group // 4)],
                          None, one_in_sem.at[group // 4]).wait_recv()
                forward_one(group).start()

    def launch(group):
        sends(group, early, lambda copy: copy.start())
        if late:
            @pl.when(quad != 2)
            def _():
                sends(group, late, lambda copy: copy.start())

    for block in blocks:
        @pl.when(me + block >= axis)
        def _():
            recv_refs[block - 1][...] = jnp.zeros_like(recv_refs[block - 1])
            got_refs[block - 1][...] = jnp.zeros_like(got_refs[block - 1])
    flag_buf[0] = flag_ref[...]
    for found in found_refs:
        found[...] = jnp.zeros_like(found)
    flux_copy.wait()

    total_slots = caps[0] + sum(slots[1:])
    starts = [0, caps[0]]
    for block in blocks:
        starts.append(starts[-1] + slots[block])
    bases = [sum(caps[:block]) for block in range(reach + 1)]

    def columns(group):
        return pl.ds(pl.multiple_of(group * wide, wide), wide)

    def local_out(group, slot):
        return pltpu.make_async_copy(local_buf.at[slot], dense_ref.at[pl.ds(0, caps[0]), columns(group)], local_sem.at[slot])

    def dense_out(group, slot):
        return pltpu.make_async_copy(
            dense_buf.at[slot], dense_ref.at[pl.ds(caps[0], sum(caps[1:])), columns(group)], dense_sem.at[slot])

    def accumulate(block, group, rows):
        found_refs[block][...] += contract(flux_ref[:, columns(group)], rows, 1, 1)

    lead = min(2, groups)

    def pack(group, carry):
        slot = lax.rem(group, 2)
        fetch(group, slot).wait()

        @pl.when(group + 1 < groups)
        def _():
            fetch(group + 1, 1 - slot).start()

        @pl.when(group >= 2)
        def _():
            local_out(group - 2, slot).wait()

        @pl.when(group >= 1)
        def _():
            launch(group - 1)

        prints = prints_buf[slot].reshape(prints_buf.shape[1] * prints_buf.shape[2], wide)
        slot_ids = lax.broadcasted_iota(jnp.int32, (total_slots, 1), 0).astype(F32)
        for half in range(GROUP):
            tile = group * GROUP + half
            select = (slot_ids == pos_ref[pl.ds(tile, 1), :]).astype(F32).astype(BF16)
            packed = jnp.dot(select, prints[:, half * 128 : (half + 1) * 128], preferred_element_type=F32).astype(BF16)
            local_buf[slot, :, half * 128 : (half + 1) * 128] = packed[: caps[0]]
            for block in blocks:
                send_refs[block - 1][tile] = packed[starts[block] : starts[block + 1]]
        local_out(group, slot).start()
        accumulate(0, group, local_buf[slot])

        @pl.when(group >= groups - lead)
        def _():
            relay(group - (groups - lead))
        return carry

    lax.fori_loop(0, groups, pack, 0)
    launch(groups - 1)
    for group in range(max(0, groups - 2), groups):
        local_out(group, group % 2).wait()

    for block in blocks:
        @pl.when(me + block < axis)
        def _():
            meta_copy(block, me).wait_recv()
        meta = got_refs[block - 1][...].astype(F32)
        top = meta[:tiles]
        top = jnp.concatenate([top, jnp.zeros((128 - tiles, top.shape[1]), F32)], axis=0)
        column_refs[block - 1][...] = top.T.astype(BF16)


    def unpack(group, carry):
        slot = lax.rem(group, 2)

        @pl.when(group + lead < groups)
        def _():
            relay(group + lead)

        def flag_copy(index):
            target = {"cells": 1 - core} if index == len(hops) else to(flip(hops[index]))
            return remote(flag_buf.at[index], flag_in.at[index], flag_sem.at[0, index], flag_sem.at[1, index], target)

        for index in range(len(hops) + 1):
            @pl.when(group == 2 * index)
            def _():
                flag_copy(index).start()

            @pl.when(group == 2 * index + 1)
            def _():
                flag_copy(index).wait()
                merged = jnp.maximum(flag_buf[index], flag_in[index])
                flag_buf[index + 1] = merged

        @pl.when(group >= 2)
        def _():
            dense_out(group - 2, slot).wait()

        for block in blocks:
            @pl.when(me + block < axis)
            def _():
                bulk_copy(block, group, send_refs[block - 1].at[part_of(group)], me).wait_recv()
            low = bases[block] - caps[0]
            for half in range(GROUP):
                tile = group * GROUP + half
                pick = lax.broadcasted_iota(jnp.int32, (128, slots[block]), 0) == tile
                spread = jnp.dot(column_refs[block - 1][...], pick.astype(F32).astype(BF16), preferred_element_type=F32)
                ids = lax.broadcasted_iota(jnp.int32, (1, slots[block]), 1).astype(F32) + 1.0
                place = (spread == ids).astype(F32).astype(BF16)
                rows = jnp.dot(place, recv_refs[block - 1][tile], preferred_element_type=F32).astype(BF16)
                dense_buf[slot, low : low + caps[block], half * 128 : (half + 1) * 128] = rows
            accumulate(block, group, dense_buf[slot, low : low + caps[block], :])
        dense_out(group, slot).start()
        return carry

    lax.fori_loop(0, groups, unpack, 0)
    for group in range(max(0, groups - 2), groups):
        dense_out(group, group % 2).wait()
    flag_out[...] = flag_buf[len(hops) + 1]

    def table(block):
        return meta_refs[0] if block == 0 else got_refs[block - 1]

    def owners(block):
        ids = table(block)[tiles + hours : tiles + hours + 8, :].astype(F32)[:1]
        rows = lax.broadcasted_iota(jnp.int32, (obs, caps[block]), 0).astype(F32) + 1.0
        return (rows == ids).astype(F32).astype(BF16)

    def partial_of(block):
        match = table(block)[tiles : tiles + hours, :].astype(F32)
        found = found_refs[block][...].reshape(samples, hours, caps[block])
        return split_dot(jnp.sum(found * match[None], axis=1), owners(block), 1, 1)

    def part_copy(block, target):
        return remote(part_own.at[block - 1], part_in.at[block - 1], part_send.at[block - 1], part_recv.at[block - 1], to(target))

    for block in reversed(blocks):
        part_own[block - 1] = partial_of(block)
    total = partial_of(0)
    for block in reversed(blocks):
        @pl.when(me + block < axis)
        def _():
            part_copy(block, me + block).start()

        @pl.when(me < block)
        def _():
            part_in[block - 1] = jnp.zeros((samples, obs), F32)
    for block in blocks:
        @pl.when(me >= block)
        def _():
            part_copy(block, me).wait_recv()
        total = total + part_in[block - 1]
    total_buf[...] = total
    swap = remote(total_buf, other_buf, core_sem.at[0], core_sem.at[1], {"cells": 1 - core})
    swap.start()
    swap.wait()
    modeled = total_buf[...] + other_buf[...]
    modeled_ref[...] = modeled
    residual = (weight_ref[...] * (modeled - value_ref[...])).astype(BF16)
    res_buf[...] = residual

    def res_copy(block, target):
        return remote(res_buf, res_in.at[block - 1], res_send.at[block - 1], res_recv.at[block - 1], to(target))

    line_refs[0][...] = contract(residual, owners(0), 1, 0).astype(BF16)
    for block in reversed(blocks):
        @pl.when(me >= block)
        def _():
            res_copy(block, me - block).start()

        @pl.when(me + block >= axis)
        def _():
            res_in[block - 1] = jnp.zeros((samples, obs), BF16)
    for block in blocks:
        match_refs[block - 1][...] = got_refs[block - 1][tiles : tiles + hours, :]
    for block in blocks:
        @pl.when(me + block < axis)
        def _():
            res_copy(block, me).wait_recv()
        line_refs[block][...] = contract(res_in[block - 1], owners(block), 1, 0).astype(BF16)

    for block in blocks:
        @pl.when(me >= block)
        def _():
            meta_copy(block, me).wait_send()
            res_copy(block, me).wait_send()

        @pl.when(me + block < axis)
        def _():
            part_copy(block, me).wait_send()

    def drain(group, carry):
        for block in blocks:
            @pl.when(me >= block)
            def _():
                bulk_copy(block, group, send_refs[block - 1].at[part_of(group)], me).wait_send()
        if relays:
            @pl.when(is_two)
            def _():
                forward_two(group).wait_send()

            @pl.when(is_one & (lax.rem(group, 4) == 3))
            def _():
                forward_one(group).wait_send()
        return carry

    lax.fori_loop(0, groups, drain, 0)


def exchange(caps, slots, flux, footprint, pos, flag, metas, obs_value, obs_weight, axis):
    samples, hours, cells = flux.shape
    obs, bands, _ = footprint.shape
    tiles = pos.shape[0]
    reach = len(caps) - 1
    groups = tiles // GROUP
    wide = GROUP * 128
    lines = samples * hours
    hop_count = max(1, math.ceil(math.log2(axis)))
    vmem = pl.BlockSpec(memory_space=pltpu.VMEM)
    anywhere = pl.BlockSpec(memory_space=pl.ANY)
    dma = pltpu.SemaphoreType.DMA
    depth = sum(caps)
    out_shape = [
        jax.ShapeDtypeStruct((depth, cells), BF16),
        jax.ShapeDtypeStruct((samples, obs), F32),
        jax.ShapeDtypeStruct((8, 128), F32),
    ]
    out_shape += [jax.ShapeDtypeStruct((samples, cap), BF16) for cap in caps]
    out_shape += [jax.ShapeDtypeStruct((hours, cap), BF16) for cap in caps[1:]]
    scratch = [
        pltpu.VMEM((2, obs, bands, wide), BF16),
        pltpu.VMEM((lines, cells), BF16),
        pltpu.VMEM((2, caps[0], wide), BF16),
        pltpu.VMEM((2, depth - caps[0], wide), BF16),
        pltpu.VMEM((reach, samples, obs), F32),
        pltpu.VMEM((reach, samples, obs), F32),
        pltpu.VMEM((samples, obs), F32),
        pltpu.VMEM((samples, obs), F32),
        pltpu.VMEM((samples, obs), BF16),
        pltpu.VMEM((reach, samples, obs), BF16),
        pltpu.VMEM((hop_count + 2, 8, 128), F32),
        pltpu.VMEM((hop_count + 1, 8, 128), F32),
    ]
    scratch += [pltpu.VMEM((tiles, slot, 128), BF16) for slot in slots[1:]] * 2
    scratch += [pltpu.VMEM((lines, cap), F32) for cap in caps]
    scratch += [pltpu.VMEM(metas[0].shape[:1] + (cap,), BF16) for cap in caps[1:]]
    scratch += [pltpu.VMEM((cap, 128), BF16) for cap in caps[1:]]
    scratch += [
        pltpu.VMEM((tiles, slots[min(2, reach)], 128), BF16),
        pltpu.VMEM((GROUP * max(1, groups // 4), slots[1], 128), BF16),
    ]
    scratch += [
        dma((2,)), dma, dma((2,)), dma((2,)),
        dma((reach, groups)), dma((reach, groups)),
        dma((groups,)), dma((groups,)), dma((max(1, groups // 4),)), dma((max(1, groups // 4),)),
        dma((reach,)), dma((reach,)), dma((reach,)), dma((reach,)),
        dma((2,)), dma((reach,)), dma((reach,)), dma((2, hop_count + 1)),
    ]
    geometry = (caps, slots, tiles, hours, axis)
    return pl.pallas_call(
        functools.partial(bulk_kernel, geometry),
        in_specs=[anywhere, anywhere] + [vmem] * (4 + len(metas)),
        out_specs=[anywhere] + [vmem] * (len(out_shape) - 1),
        out_shape=out_shape,
        scratch_shapes=scratch,
        compiler_params=pltpu.CompilerParams(
            collective_id=0, has_side_effects=True, vmem_limit_bytes=VMEM_LIMIT),
        name="bulk",
    )(footprint, flux.reshape(lines, cells), pos, flag, obs_value, obs_weight[None, :], *metas)


def adjoint_kernel(count, *refs):
    dense_ref, out_ref, line_buf = refs[2 * count], refs[2 * count + 1], refs[2 * count + 2]

    @pl.when(pl.program_id(0) == 0)
    def _():
        pieces = []
        for line, match in zip(refs[:count], refs[count : 2 * count]):
            values = line[...].astype(F32)[:, None, :] * match[...].astype(F32)[None]
            pieces.append(values.reshape(-1, values.shape[2]))
        line_buf[...] = jnp.concatenate(pieces, axis=1).astype(BF16)

    out_ref[...] = jnp.dot(line_buf[...], dense_ref[...], preferred_element_type=F32)


def adjoint(lines, matches, dense):
    depth, cells = dense.shape
    tile = min(TILE_CELLS, cells)
    height = lines[0].shape[0] * matches[0].shape[0]
    whole = [pl.BlockSpec(part.shape, lambda i: (0, 0)) for part in lines + matches]
    return pl.pallas_call(
        functools.partial(adjoint_kernel, len(lines)),
        grid=(cells // tile,),
        in_specs=whole + [pl.BlockSpec((depth, tile), lambda i: (0, i))],
        out_specs=pl.BlockSpec((height, tile), lambda i: (0, i)),
        out_shape=jax.ShapeDtypeStruct((height, cells), F32),
        scratch_shapes=[pltpu.VMEM((height, depth), BF16)],
        compiler_params=pltpu.CompilerParams(
            dimension_semantics=("arbitrary",), vmem_limit_bytes=VMEM_LIMIT),
        name="adjoint",
    )(*lines, *matches, dense)


def whole_plan(reach, flux, footprint, band_lag, obs_hour, tile_mask, obs_value, obs_weight):
    samples, hours, cells = flux.shape
    obs, bands, _ = footprint.shape
    rows = obs * bands
    position = lax.axis_index("tm")
    tiles = tile_mask.shape[1]
    source = (obs_hour[:, None] - band_lag).reshape(1, rows)
    hour_ids = lax.broadcasted_iota(jnp.int32, (hours, rows), 0)
    obs_ids = lax.broadcasted_iota(jnp.int32, (rows, obs), 0) // bands
    owner = (obs_ids == lax.broadcasted_iota(jnp.int32, (rows, obs), 1)).astype(BF16)
    masked = footprint.reshape(obs, bands, tiles, cells // tiles) * tile_mask.astype(BF16)[:, None, :, None]
    masked = masked.reshape(rows, cells)
    flux_lines = flux.reshape(samples * hours, cells)
    blocks = range(reach + 1)

    def sent(value, steps):
        return shifted(value, "tm", steps) if steps else value

    prints, matches, total = [], [], 0.0
    for block in blocks:
        match = ((source == hour_ids + (position - block) * hours) & (source >= 0)).astype(BF16)
        prints.append(sent(masked, -block))
        matches.append(sent(match, -block))
        found = contract(flux_lines, prints[block], 1, 1).reshape(samples, hours, rows)
        value = jnp.sum(found * matches[block].astype(F32)[None], axis=1)
        total = total + contract(sent(value, block), owner.astype(F32), 1, 0, precision=lax.Precision.HIGHEST)
    modeled = over_axis(total, "cells")
    residual = (obs_weight[None, :] * (modeled - obs_value)).astype(BF16)
    values = contract(residual, owner, 1, 1, BF16)
    gradient = 0.0
    for block in blocks:
        lines = sent(values, -block)[:, None, :] * matches[block][None]
        gradient = gradient + contract(lines.reshape(samples * hours, rows), prints[block], 1, 0)
    return modeled, gradient


def body(axis, flux, footprint, band_lag, obs_hour, tile_mask, obs_value, obs_weight):
    samples, hours, cells = flux.shape
    obs, bands, _ = footprint.shape
    tiles = tile_mask.shape[1]
    reach = -(-(LAGS - 1) // hours)
    sizes = [capacities(block, hours, obs, bands) for block in range(reach + 1)]
    caps = tuple(size[0] for size in sizes)
    slots = tuple(size[1] for size in sizes)
    pos, flag, *metas = prepare(caps, slots, hours, band_lag, obs_hour, tile_mask)
    outs = exchange(caps, slots, flux, footprint, pos, flag, metas, obs_value, obs_weight, axis)
    dense, modeled, flags = outs[:3]
    lines = list(outs[3 : 4 + reach])
    matches = [metas[0][tiles : tiles + hours]] + list(outs[4 + reach :])

    def slow():
        return whole_plan(reach, flux, footprint, band_lag, obs_hour, tile_mask, obs_value, obs_weight)

    def fast():
        return modeled, adjoint(lines, matches, dense)

    modeled, gradient = lax.cond(flags[0, 0] > 0, slow, fast)
    return modeled, gradient.reshape(samples, hours, cells)


def solution(mesh):
    placed = (
        P(None, "tm", "cells"),
        P("tm", None, "cells"),
        P("tm", None),
        P("tm"),
        P("tm", "cells"),
        P(None, "tm"),
        P("tm"),
    )
    return jax.shard_map(
        functools.partial(body, mesh.shape["tm"]),
        mesh=mesh,
        in_specs=placed,
        out_specs=(P(None, "tm"), P(None, "tm", "cells")),
        check_vma=False,
    )
```

```python
import functools
import math

import jax
import jax.numpy as jnp
from jax import lax
from jax.experimental import pallas as pl
from jax.experimental.pallas import tpu as pltpu
from jax.sharding import PartitionSpec as P

LAGS = 24
GRAIN = 16
GROUP = 2
UNPACK_LAG = 4
RELAY_LAG = 2
TILE_CELLS = 512
VMEM_LIMIT = 62 * 2**20
MESH = pl.DeviceIdType.MESH
BF16 = jnp.bfloat16
F32 = jnp.float32


def shifted(value, axis, steps):
    count = lax.axis_size(axis)
    initial, last = (max(0, -steps), min(count, count - steps))
    return lax.ppermute(value, axis, [(source, source + steps) for source in range(initial, last)])


def over_axis(value, axis):
    if lax.axis_size(axis) == 2:
        return value + lax.ppermute(value, axis, [(0, 1), (1, 0)])
    return lax.psum(value, axis)


def contract(left, right, left_dim, right_dim, out=F32, precision=None):
    return lax.dot_general(
        left, right, (((left_dim,), (right_dim,)), ((), ())),
        precision=precision, preferred_element_type=out,
    )


def capacities(block, hours, obs, bands):
    mean = spread = mean_square = 0.0
    for hour in range(hours):
        hits = sum(1 for lag in range(LAGS) if (hour - lag) // hours == -block)
        share = hits / LAGS
        mean += bands * share / hours
        mean_square += (bands * share) ** 2 / hours
        spread += bands * share * (1 - share) * (LAGS - bands) / (LAGS - 1) / hours
    spread += mean_square - mean**2
    rows = obs * mean + 4.0 * math.sqrt(obs * spread)
    half_spread = 0.5 * (spread + mean**2) - 0.25 * mean**2
    slots = 0.5 * obs * mean + 4.7 * math.sqrt(obs * half_spread)
    rows = min(obs * bands, GRAIN * math.ceil(rows / GRAIN))
    return rows, min(rows, GRAIN * math.ceil(slots / GRAIN))


def prep_kernel(caps, slots, lag_ref, hour_ref, mask_ref, band_ref, pos_ref, flag_ref, *meta_refs):
    reach = len(caps) - 1
    bands, obs = lag_ref.shape
    tiles = mask_ref.shape[0]
    rows = bands * obs
    hours = meta_refs[0].shape[0] - tiles - 8
    position = lax.axis_index("tm")
    first = (position - reach) * hours
    row_ids = lax.broadcasted_iota(jnp.int32, (obs, rows), 1)
    obs_ids = lax.broadcasted_iota(jnp.int32, (obs, rows), 0)
    spread = ((row_ids >= obs_ids * bands) & (row_ids < (obs_ids + 1) * bands)).astype(F32).astype(BF16)
    ahead = hour_ref[...] - lag_ref[...] - first
    ahead = jnp.concatenate([ahead, jnp.zeros((8 - bands % 8, obs), jnp.int32)], axis=0) if bands % 8 else ahead
    ahead = jnp.dot(ahead.astype(F32).astype(BF16), spread, preferred_element_type=F32)
    ahead = jnp.sum(ahead * band_ref[...], axis=0, keepdims=True)
    on = jnp.dot(mask_ref[...].astype(F32).astype(BF16), spread, preferred_element_type=F32)
    ids = lax.broadcasted_iota(jnp.int32, (8, obs), 1).astype(F32) + 1.0
    ids = jnp.dot(ids.astype(BF16), spread, preferred_element_type=F32)[:1]
    valid = ahead >= (-first).astype(F32)
    members, lines = [], []
    for block in range(reach + 1):
        low = hours * (reach - block)
        member = (ahead >= low) & (ahead < low + hours) & valid
        members.append(member.astype(F32))
    head = jnp.concatenate(members + [jnp.zeros((8 - (reach + 1) % 8, rows), F32)], axis=0)
    lines = [head] + [members[block] * on for block in range(1, reach + 1)]
    before = lax.broadcasted_iota(jnp.int32, (rows, rows), 0) < lax.broadcasted_iota(jnp.int32, (rows, rows), 1)
    before = before.astype(F32).astype(BF16)
    ranks = jnp.dot(jnp.concatenate(lines, axis=0).astype(BF16), before, preferred_element_type=F32)
    over = jnp.zeros((1, rows), F32)
    pos = jnp.full((tiles, rows), -1.0, F32)
    base = caps[0]
    for block in range(reach + 1):
        member = members[block]
        rank = ranks[block : block + 1]
        over = jnp.maximum(over, jnp.where((member > 0) & (rank >= caps[block]), 1.0, 0.0))
        row_slot = jnp.where(member > 0, rank, -1.0)
        if block == 0:
            pos = jnp.where((member * on > 0) & (rank < caps[0]), rank, pos)
            order = jnp.zeros((tiles, rows), F32)
        else:
            start = head.shape[0] + (block - 1) * tiles
            tile_rank = ranks[start : start + tiles]
            inside = member * on > 0
            excess = jnp.where(inside & (tile_rank >= slots[block]), 1.0, 0.0)
            over = jnp.maximum(over, jnp.max(excess, axis=0, keepdims=True))
            pos = jnp.where(inside & (tile_rank < slots[block]), tile_rank + base, pos)
            order = jnp.where(inside, tile_rank + 1.0, 0.0)
            base += slots[block]
        hour_of = lax.broadcasted_iota(jnp.int32, (hours, rows), 0).astype(F32) + float(hours * (reach - block))
        match = jnp.where((ahead == hour_of) & valid, 1.0, 0.0)
        tail = jnp.where(lax.broadcasted_iota(jnp.int32, (8, rows), 0) == 0, ids, 0.0)
        values = jnp.concatenate([order, match, tail], axis=0).astype(BF16)
        select = lax.broadcasted_iota(jnp.int32, (caps[block], rows), 0).astype(F32) == row_slot
        select = select.astype(F32).astype(BF16)
        meta_refs[block][...] = contract(values, select, 1, 1).astype(BF16)
    pos_ref[...] = pos
    flag_ref[...] = jnp.broadcast_to(jnp.max(over, axis=1, keepdims=True), (8, 128))


def prepare(caps, slots, hours, band_lag, obs_hour, tile_mask):
    obs, bands = band_lag.shape
    tiles = tile_mask.shape[1]
    rows = obs * bands
    pad = bands + (8 - bands % 8 if bands % 8 else 0)
    band = (jnp.arange(rows) % bands == jnp.arange(pad)[:, None]).astype(F32)
    vmem = pl.BlockSpec(memory_space=pltpu.VMEM)
    shapes = [
        jax.ShapeDtypeStruct((tiles, rows), F32),
        jax.ShapeDtypeStruct((8, 128), F32),
    ] + [jax.ShapeDtypeStruct((tiles + hours + 8, cap), BF16) for cap in caps]
    return pl.pallas_call(
        functools.partial(prep_kernel, caps, slots),
        in_specs=[vmem] * 4,
        out_specs=[vmem] * len(shapes),
        out_shape=shapes,
        compiler_params=pltpu.CompilerParams(vmem_limit_bytes=VMEM_LIMIT),
        name="prep",
    )(band_lag.T, obs_hour[None, :], tile_mask.T, band)


def split_dot(left, right, left_dim, right_dim):
    total = None
    for _ in range(3):
        term = left.astype(BF16)
        left = left - term.astype(F32)
        part = contract(term, right, left_dim, right_dim)
        total = part if total is None else total + part
    return total


def bulk_kernel(geometry, *refs):
    caps, slots, tiles, hours, axis = geometry
    reach = len(caps) - 1
    blocks = range(1, reach + 1)
    refs = list(refs)

    def take(count):
        head = refs[:count]
        del refs[:count]
        return head

    (prints_ref, flux_hbm, pos_ref, flag_ref, value_ref, weight_ref) = take(6)
    meta_refs = take(reach + 1)
    (dense_ref, modeled_ref, flag_out) = take(3)
    line_refs = take(reach + 1)
    match_refs = take(reach)
    (prints_buf, flux_ref, local_buf, dense_buf, part_own, part_in, total_buf, other_buf,
     res_buf, res_in, flag_buf, flag_in) = take(12)
    send_refs, recv_refs, found_refs, got_refs, column_refs = (
        take(reach), take(reach), take(reach + 1), take(reach), take(reach))
    (relay_ref, relay_one) = take(2)
    (prints_sem, flux_sem, local_sem, dense_sem, send_sem, recv_sem, relay_in_sem, relay_out_sem,
     one_in_sem, one_out_sem, meta_send, meta_recv, part_send, part_recv, core_sem, res_send, res_recv,
     flag_sem) = take(18)

    me = lax.axis_index("tm")
    core = lax.axis_index("cells")
    obs = value_ref.shape[1]
    samples = value_ref.shape[0]
    groups = tiles // GROUP
    wide = GROUP * 128
    quad = lax.rem(me, 4)
    relays = axis % 4 == 0 and reach >= 2

    def to(tm):
        return {"tm": tm}

    partners = [step for step in (1, 2, 3, 4) if step < axis]
    hops = []
    step = 1
    while step < axis:
        hops.append(step)
        step *= 2
    far = [hop for hop in hops if hop > 4]

    def flip(hop):
        return jnp.where(lax.rem(me // hop, 2) == 0, me + hop, me - hop)

    barrier = pltpu.get_barrier_semaphore()
    count = jnp.int32(0)
    for step in partners:
        for target, exists in ((me + step, me + step < axis), (me - step, me >= step)):
            @pl.when(exists)
            def _():
                pl.semaphore_signal(barrier, inc=1, device_id=to(target), device_id_type=MESH)
            count = count + exists.astype(jnp.int32)
    for hop in far:
        pl.semaphore_signal(barrier, inc=1, device_id=to(flip(hop)), device_id_type=MESH)
        count = count + 1
    pl.semaphore_signal(barrier, inc=1, device_id={"cells": 1 - core}, device_id_type=MESH)
    count = count + 1

    def fetch(group, slot):
        return pltpu.make_async_copy(
            prints_ref.at[:, :, pl.ds(pl.multiple_of(group * wide, wide), wide)],
            prints_buf.at[slot], prints_sem.at[slot])

    fetch(0, 0).start()
    flux_copy = pltpu.make_async_copy(flux_hbm, flux_ref, flux_sem)
    flux_copy.start()
    pl.semaphore_wait(barrier, count)

    def remote(src, dst, ssem, rsem, target):
        return pltpu.make_async_remote_copy(
            src_ref=src, dst_ref=dst, send_sem=ssem, recv_sem=rsem,
            device_id=target, device_id_type=MESH)

    def meta_copy(block, target):
        return remote(meta_refs[block], got_refs[block - 1], meta_send.at[block - 1], meta_recv.at[block - 1], to(target))

    for block in blocks:
        @pl.when(me >= block)
        def _():
            meta_copy(block, me - block).start()

    def part_of(group):
        return pl.ds(group * GROUP, GROUP)

    def bulk_copy(block, group, source, target, dst=None, ssem=None, rsem=None):
        return remote(source, recv_refs[block - 1].at[part_of(group)] if dst is None else dst,
                      send_sem.at[block - 1, group] if ssem is None else ssem,
                      recv_sem.at[block - 1, group] if rsem is None else rsem, to(target))

    def send(block, group):
        source = send_refs[block - 1].at[part_of(group)]
        exists = me >= block
        detour = None
        if relays and block == 2:
            detour = (quad == 0) & (lax.rem(group, 2) == 1)
            copy = bulk_copy(2, group, source, me + 2, relay_ref.at[part_of(group)], None, relay_in_sem.at[group])
        elif relays and block == 1:
            detour = (lax.rem(me, 2) == 0) & (lax.rem(group, 4) == 2)
            copy = bulk_copy(1, group, source, jnp.where(quad == 0, me + 2, me - 2),
                             relay_one.at[part_of(group // 4)], None, one_in_sem.at[group // 4])
        if detour is None:
            @pl.when(exists)
            def _():
                bulk_copy(block, group, source, me - block).start()
        else:
            @pl.when(exists & detour)
            def _():
                copy.start()

            @pl.when(exists & jnp.logical_not(detour))
            def _():
                bulk_copy(block, group, source, me - block).start()

    def forward_two(group):
        return bulk_copy(2, group, relay_ref.at[part_of(group)], me - 4, None, relay_out_sem.at[group])

    def forward_one(group):
        return bulk_copy(1, group, relay_one.at[part_of(group // 4)], jnp.where(quad == 0, me + 1, me - 3),
                         None, one_out_sem.at[group // 4])

    is_two = (quad == 2) & (me >= 6)
    is_one = (lax.rem(me, 2) == 0) & (me != 2)
    def relay(group):
        if relays:
            @pl.when(is_two & (lax.rem(group, 2) == 1))
            def _():
                bulk_copy(2, group, send_refs[1].at[part_of(group)], me - 4, relay_ref.at[part_of(group)],
                          None, relay_in_sem.at[group]).wait_recv()
                forward_two(group).start()

            @pl.when(is_one & (lax.rem(group, 4) == 2))
            def _():
                bulk_copy(1, group, send_refs[0].at[part_of(group)], me, relay_one.at[part_of(group // 4)],
                          None, one_in_sem.at[group // 4]).wait_recv()
                forward_one(group).start()

    def launch(group):
        for block in blocks:
            send(block, group)

    for block in blocks:
        @pl.when(me + block >= axis)
        def _():
            recv_refs[block - 1][...] = jnp.zeros_like(recv_refs[block - 1])
            got_refs[block - 1][...] = jnp.zeros_like(got_refs[block - 1])
    flag_buf[0] = flag_ref[...]
    for found in found_refs:
        found[...] = jnp.zeros_like(found)
    flux_copy.wait()

    total_slots = caps[0] + sum(slots[1:])
    starts = [0, caps[0]]
    for block in blocks:
        starts.append(starts[-1] + slots[block])
    bases = [sum(caps[:block]) for block in range(reach + 1)]

    def columns(group):
        return pl.ds(pl.multiple_of(group * wide, wide), wide)

    def local_out(group, slot):
        return pltpu.make_async_copy(local_buf.at[slot], dense_ref.at[pl.ds(0, caps[0]), columns(group)], local_sem.at[slot])

    def dense_out(group, slot):
        return pltpu.make_async_copy(
            dense_buf.at[slot], dense_ref.at[pl.ds(caps[0], sum(caps[1:])), columns(group)], dense_sem.at[slot])

    def accumulate(block, group, rows):
        found_refs[block][...] += contract(flux_ref[:, columns(group)], rows, 1, 1)

    def pack(group):
        slot = lax.rem(group, 2)
        fetch(group, slot).wait()

        @pl.when(group + 1 < groups)
        def _():
            fetch(group + 1, 1 - slot).start()

        @pl.when(group >= 2)
        def _():
            local_out(group - 2, slot).wait()

        @pl.when(group >= 1)
        def _():
            launch(group - 1)

        prints = prints_buf[slot].reshape(prints_buf.shape[1] * prints_buf.shape[2], wide)
        slot_ids = lax.broadcasted_iota(jnp.int32, (total_slots, 1), 0).astype(F32)
        for half in range(GROUP):
            tile = group * GROUP + half
            select = (slot_ids == pos_ref[pl.ds(tile, 1), :]).astype(F32).astype(BF16)
            packed = jnp.dot(select, prints[:, half * 128 : (half + 1) * 128], preferred_element_type=F32).astype(BF16)
            local_buf[slot, :, half * 128 : (half + 1) * 128] = packed[: caps[0]]
            for block in blocks:
                send_refs[block - 1][tile] = packed[starts[block] : starts[block + 1]]
        local_out(group, slot).start()
        accumulate(0, group, local_buf[slot])

    def receive_tables():
        for block in blocks:
            @pl.when(me + block < axis)
            def _():
                meta_copy(block, me).wait_recv()
            meta = got_refs[block - 1][...].astype(F32)
            top = meta[:tiles]
            top = jnp.concatenate([top, jnp.zeros((128 - tiles, top.shape[1]), F32)], axis=0)
            column_refs[block - 1][...] = top.T.astype(BF16)


    def unpack(group):
        slot = lax.rem(group, 2)

        def flag_copy(index):
            target = {"cells": 1 - core} if index == len(hops) else to(flip(hops[index]))
            return remote(flag_buf.at[index], flag_in.at[index], flag_sem.at[0, index], flag_sem.at[1, index], target)

        for index in range(len(hops) + 1):
            @pl.when(group == 2 * index)
            def _():
                flag_copy(index).start()

            @pl.when(group == 2 * index + 1)
            def _():
                flag_copy(index).wait()
                merged = jnp.maximum(flag_buf[index], flag_in[index])
                flag_buf[index + 1] = merged

        @pl.when(group >= 2)
        def _():
            dense_out(group - 2, slot).wait()

        for block in blocks:
            @pl.when(me + block < axis)
            def _():
                bulk_copy(block, group, send_refs[block - 1].at[part_of(group)], me).wait_recv()
            low = bases[block] - caps[0]
            for half in range(GROUP):
                tile = group * GROUP + half
                pick = lax.broadcasted_iota(jnp.int32, (128, slots[block]), 0) == tile
                spread = jnp.dot(column_refs[block - 1][...], pick.astype(F32).astype(BF16), preferred_element_type=F32)
                ids = lax.broadcasted_iota(jnp.int32, (1, slots[block]), 1).astype(F32) + 1.0
                place = (spread == ids).astype(F32).astype(BF16)
                rows = jnp.dot(place, recv_refs[block - 1][tile], preferred_element_type=F32).astype(BF16)
                dense_buf[slot, low : low + caps[block], half * 128 : (half + 1) * 128] = rows
            accumulate(block, group, dense_buf[slot, low : low + caps[block], :])
        dense_out(group, slot).start()

    def step_through(index, carry):
        @pl.when(index < groups)
        def _():
            pack(index)

        @pl.when(index == groups)
        def _():
            launch(groups - 1)

        @pl.when((index >= RELAY_LAG) & (index < groups + RELAY_LAG))
        def _():
            relay(index - RELAY_LAG)

        @pl.when(index == UNPACK_LAG)
        def _():
            receive_tables()

        @pl.when(index >= UNPACK_LAG)
        def _():
            unpack(index - UNPACK_LAG)
        return carry

    lax.fori_loop(0, groups + UNPACK_LAG, step_through, 0)
    for group in range(max(0, groups - 2), groups):
        local_out(group, group % 2).wait()
    for group in range(max(0, groups - 2), groups):
        dense_out(group, group % 2).wait()
    flag_out[...] = flag_buf[len(hops) + 1]

    def table(block):
        return meta_refs[0] if block == 0 else got_refs[block - 1]

    def owners(block):
        ids = table(block)[tiles + hours : tiles + hours + 8, :].astype(F32)[:1]
        rows = lax.broadcasted_iota(jnp.int32, (obs, caps[block]), 0).astype(F32) + 1.0
        return (rows == ids).astype(F32).astype(BF16)

    def partial_of(block):
        match = table(block)[tiles : tiles + hours, :].astype(F32)
        found = found_refs[block][...].reshape(samples, hours, caps[block])
        return split_dot(jnp.sum(found * match[None], axis=1), owners(block), 1, 1)

    def part_copy(block, target):
        return remote(part_own.at[block - 1], part_in.at[block - 1], part_send.at[block - 1], part_recv.at[block - 1], to(target))

    for block in reversed(blocks):
        part_own[block - 1] = partial_of(block)
    total = partial_of(0)
    for block in reversed(blocks):
        @pl.when(me + block < axis)
        def _():
            part_copy(block, me + block).start()

        @pl.when(me < block)
        def _():
            part_in[block - 1] = jnp.zeros((samples, obs), F32)
    for block in blocks:
        @pl.when(me >= block)
        def _():
            part_copy(block, me).wait_recv()
        total = total + part_in[block - 1]
    total_buf[...] = total
    swap = remote(total_buf, other_buf, core_sem.at[0], core_sem.at[1], {"cells": 1 - core})
    swap.start()
    swap.wait()
    modeled = total_buf[...] + other_buf[...]
    modeled_ref[...] = modeled
    residual = (weight_ref[...] * (modeled - value_ref[...])).astype(BF16)
    res_buf[...] = residual

    def res_copy(block, target):
        return remote(res_buf, res_in.at[block - 1], res_send.at[block - 1], res_recv.at[block - 1], to(target))

    line_refs[0][...] = contract(residual, owners(0), 1, 0).astype(BF16)
    for block in reversed(blocks):
        @pl.when(me >= block)
        def _():
            res_copy(block, me - block).start()

        @pl.when(me + block >= axis)
        def _():
            res_in[block - 1] = jnp.zeros((samples, obs), BF16)
    for block in blocks:
        match_refs[block - 1][...] = got_refs[block - 1][tiles : tiles + hours, :]
    for block in blocks:
        @pl.when(me + block < axis)
        def _():
            res_copy(block, me).wait_recv()
        line_refs[block][...] = contract(res_in[block - 1], owners(block), 1, 0).astype(BF16)

    for block in blocks:
        @pl.when(me >= block)
        def _():
            meta_copy(block, me).wait_send()
            res_copy(block, me).wait_send()

        @pl.when(me + block < axis)
        def _():
            part_copy(block, me).wait_send()

    def drain(group, carry):
        for block in blocks:
            @pl.when(me >= block)
            def _():
                bulk_copy(block, group, send_refs[block - 1].at[part_of(group)], me).wait_send()
        if relays:
            @pl.when(is_two & (lax.rem(group, 2) == 1))
            def _():
                forward_two(group).wait_send()

            @pl.when(is_one & (lax.rem(group, 4) == 2))
            def _():
                forward_one(group).wait_send()
        return carry

    lax.fori_loop(0, groups, drain, 0)


def exchange(caps, slots, flux, footprint, pos, flag, metas, obs_value, obs_weight, axis):
    samples, hours, cells = flux.shape
    obs, bands, _ = footprint.shape
    tiles = pos.shape[0]
    reach = len(caps) - 1
    groups = tiles // GROUP
    wide = GROUP * 128
    lines = samples * hours
    hop_count = max(1, math.ceil(math.log2(axis)))
    vmem = pl.BlockSpec(memory_space=pltpu.VMEM)
    anywhere = pl.BlockSpec(memory_space=pl.ANY)
    dma = pltpu.SemaphoreType.DMA
    depth = sum(caps)
    out_shape = [
        jax.ShapeDtypeStruct((depth, cells), BF16),
        jax.ShapeDtypeStruct((samples, obs), F32),
        jax.ShapeDtypeStruct((8, 128), F32),
    ]
    out_shape += [jax.ShapeDtypeStruct((samples, cap), BF16) for cap in caps]
    out_shape += [jax.ShapeDtypeStruct((hours, cap), BF16) for cap in caps[1:]]
    scratch = [
        pltpu.VMEM((2, obs, bands, wide), BF16),
        pltpu.VMEM((lines, cells), BF16),
        pltpu.VMEM((2, caps[0], wide), BF16),
        pltpu.VMEM((2, depth - caps[0], wide), BF16),
        pltpu.VMEM((reach, samples, obs), F32),
        pltpu.VMEM((reach, samples, obs), F32),
        pltpu.VMEM((samples, obs), F32),
        pltpu.VMEM((samples, obs), F32),
        pltpu.VMEM((samples, obs), BF16),
        pltpu.VMEM((reach, samples, obs), BF16),
        pltpu.VMEM((hop_count + 2, 8, 128), F32),
        pltpu.VMEM((hop_count + 1, 8, 128), F32),
    ]
    scratch += [pltpu.VMEM((tiles, slot, 128), BF16) for slot in slots[1:]] * 2
    scratch += [pltpu.VMEM((lines, cap), F32) for cap in caps]
    scratch += [pltpu.VMEM(metas[0].shape[:1] + (cap,), BF16) for cap in caps[1:]]
    scratch += [pltpu.VMEM((cap, 128), BF16) for cap in caps[1:]]
    scratch += [
        pltpu.VMEM((tiles, slots[min(2, reach)], 128), BF16),
        pltpu.VMEM((GROUP * max(1, groups // 4), slots[1], 128), BF16),
    ]
    scratch += [
        dma((2,)), dma, dma((2,)), dma((2,)),
        dma((reach, groups)), dma((reach, groups)),
        dma((groups,)), dma((groups,)), dma((max(1, groups // 4),)), dma((max(1, groups // 4),)),
        dma((reach,)), dma((reach,)), dma((reach,)), dma((reach,)),
        dma((2,)), dma((reach,)), dma((reach,)), dma((2, hop_count + 1)),
    ]
    geometry = (caps, slots, tiles, hours, axis)
    return pl.pallas_call(
        functools.partial(bulk_kernel, geometry),
        in_specs=[anywhere, anywhere] + [vmem] * (4 + len(metas)),
        out_specs=[anywhere] + [vmem] * (len(out_shape) - 1),
        out_shape=out_shape,
        scratch_shapes=scratch,
        compiler_params=pltpu.CompilerParams(
            collective_id=0, has_side_effects=True, vmem_limit_bytes=VMEM_LIMIT),
        name="bulk",
    )(footprint, flux.reshape(lines, cells), pos, flag, obs_value, obs_weight[None, :], *metas)


def adjoint_kernel(count, *refs):
    dense_ref, out_ref, line_buf = refs[2 * count], refs[2 * count + 1], refs[2 * count + 2]

    @pl.when(pl.program_id(0) == 0)
    def _():
        pieces = []
        for line, match in zip(refs[:count], refs[count : 2 * count]):
            values = line[...].astype(F32)[:, None, :] * match[...].astype(F32)[None]
            pieces.append(values.reshape(-1, values.shape[2]))
        line_buf[...] = jnp.concatenate(pieces, axis=1).astype(BF16)

    out_ref[...] = jnp.dot(line_buf[...], dense_ref[...], preferred_element_type=F32)


def adjoint(lines, matches, dense):
    depth, cells = dense.shape
    tile = min(TILE_CELLS, cells)
    height = lines[0].shape[0] * matches[0].shape[0]
    whole = [pl.BlockSpec(part.shape, lambda i: (0, 0)) for part in lines + matches]
    return pl.pallas_call(
        functools.partial(adjoint_kernel, len(lines)),
        grid=(cells // tile,),
        in_specs=whole + [pl.BlockSpec((depth, tile), lambda i: (0, i))],
        out_specs=pl.BlockSpec((height, tile), lambda i: (0, i)),
        out_shape=jax.ShapeDtypeStruct((height, cells), F32),
        scratch_shapes=[pltpu.VMEM((height, depth), BF16)],
        compiler_params=pltpu.CompilerParams(
            dimension_semantics=("arbitrary",), vmem_limit_bytes=VMEM_LIMIT),
        name="adjoint",
    )(*lines, *matches, dense)


def whole_plan(reach, flux, footprint, band_lag, obs_hour, tile_mask, obs_value, obs_weight):
    samples, hours, cells = flux.shape
    obs, bands, _ = footprint.shape
    rows = obs * bands
    position = lax.axis_index("tm")
    tiles = tile_mask.shape[1]
    source = (obs_hour[:, None] - band_lag).reshape(1, rows)
    hour_ids = lax.broadcasted_iota(jnp.int32, (hours, rows), 0)
    obs_ids = lax.broadcasted_iota(jnp.int32, (rows, obs), 0) // bands
    owner = (obs_ids == lax.broadcasted_iota(jnp.int32, (rows, obs), 1)).astype(BF16)
    masked = footprint.reshape(obs, bands, tiles, cells // tiles) * tile_mask.astype(BF16)[:, None, :, None]
    masked = masked.reshape(rows, cells)
    flux_lines = flux.reshape(samples * hours, cells)
    blocks = range(reach + 1)

    def sent(value, steps):
        return shifted(value, "tm", steps) if steps else value

    prints, matches, total = [], [], 0.0
    for block in blocks:
        match = ((source == hour_ids + (position - block) * hours) & (source >= 0)).astype(BF16)
        prints.append(sent(masked, -block))
        matches.append(sent(match, -block))
        found = contract(flux_lines, prints[block], 1, 1).reshape(samples, hours, rows)
        value = jnp.sum(found * matches[block].astype(F32)[None], axis=1)
        total = total + contract(sent(value, block), owner.astype(F32), 1, 0, precision=lax.Precision.HIGHEST)
    modeled = over_axis(total, "cells")
    residual = (obs_weight[None, :] * (modeled - obs_value)).astype(BF16)
    values = contract(residual, owner, 1, 1, BF16)
    gradient = 0.0
    for block in blocks:
        lines = sent(values, -block)[:, None, :] * matches[block][None]
        gradient = gradient + contract(lines.reshape(samples * hours, rows), prints[block], 1, 0)
    return modeled, gradient


def body(axis, flux, footprint, band_lag, obs_hour, tile_mask, obs_value, obs_weight):
    samples, hours, cells = flux.shape
    obs, bands, _ = footprint.shape
    tiles = tile_mask.shape[1]
    reach = -(-(LAGS - 1) // hours)
    sizes = [capacities(block, hours, obs, bands) for block in range(reach + 1)]
    caps = tuple(size[0] for size in sizes)
    slots = tuple(size[1] for size in sizes)
    pos, flag, *metas = prepare(caps, slots, hours, band_lag, obs_hour, tile_mask)
    outs = exchange(caps, slots, flux, footprint, pos, flag, metas, obs_value, obs_weight, axis)
    dense, modeled, flags = outs[:3]
    lines = list(outs[3 : 4 + reach])
    matches = [metas[0][tiles : tiles + hours]] + list(outs[4 + reach :])

    def slow():
        return whole_plan(reach, flux, footprint, band_lag, obs_hour, tile_mask, obs_value, obs_weight)

    def fast():
        return modeled, adjoint(lines, matches, dense)

    modeled, gradient = lax.cond(flags[0, 0] > 0, slow, fast)
    return modeled, gradient.reshape(samples, hours, cells)


def solution(mesh):
    placed = (
        P(None, "tm", "cells"),
        P("tm", None, "cells"),
        P("tm", None),
        P("tm"),
        P("tm", "cells"),
        P(None, "tm"),
        P("tm"),
    )
    return jax.shard_map(
        functools.partial(body, mesh.shape["tm"]),
        mesh=mesh,
        in_specs=placed,
        out_specs=(P(None, "tm"), P(None, "tm", "cells")),
        check_vma=False,
    )
```

```python
import functools
import math

import jax
import jax.numpy as jnp
from jax import lax
from jax.experimental import pallas as pl
from jax.experimental.pallas import tpu as pltpu
from jax.sharding import PartitionSpec as P

LAGS = 24
GRAIN = 16
GROUP = 2
UNPACK_LAG = 4
RELAY_LAG = 3
TILE_CELLS = 1024
VMEM_LIMIT = 62 * 2**20
MESH = pl.DeviceIdType.MESH
BF16 = jnp.bfloat16
F32 = jnp.float32


def shifted(value, axis, steps):
    count = lax.axis_size(axis)
    initial, last = (max(0, -steps), min(count, count - steps))
    return lax.ppermute(value, axis, [(source, source + steps) for source in range(initial, last)])


def over_axis(value, axis):
    if lax.axis_size(axis) == 2:
        return value + lax.ppermute(value, axis, [(0, 1), (1, 0)])
    return lax.psum(value, axis)


def contract(left, right, left_dim, right_dim, out=F32, precision=None):
    return lax.dot_general(
        left, right, (((left_dim,), (right_dim,)), ((), ())),
        precision=precision, preferred_element_type=out,
    )


def capacities(block, hours, obs, bands):
    mean = spread = mean_square = 0.0
    for hour in range(hours):
        hits = sum(1 for lag in range(LAGS) if (hour - lag) // hours == -block)
        share = hits / LAGS
        mean += bands * share / hours
        mean_square += (bands * share) ** 2 / hours
        spread += bands * share * (1 - share) * (LAGS - bands) / (LAGS - 1) / hours
    spread += mean_square - mean**2
    rows = obs * mean + 4.0 * math.sqrt(obs * spread)
    half_spread = 0.5 * (spread + mean**2) - 0.25 * mean**2
    slots = 0.5 * obs * mean + 4.7 * math.sqrt(obs * half_spread)
    pair_spread = 1.5 * (spread + mean**2) - mean**2
    pairs = obs * mean + 4.65 * math.sqrt(obs * pair_spread)
    rows = min(obs * bands, GRAIN * math.ceil(rows / GRAIN))
    slots = min(rows, GRAIN * math.ceil(slots / GRAIN))
    return rows, slots, max(slots, min(2 * slots, GRAIN * math.ceil(pairs / GRAIN)))


def prep_kernel(caps, slots, pairs, lag_ref, hour_ref, mask_ref, band_ref, pos_ref, flag_ref, *meta_refs):
    reach = len(caps) - 1
    bands, obs = lag_ref.shape
    tiles = mask_ref.shape[0]
    rows = bands * obs
    hours = meta_refs[0].shape[0] - tiles - 8
    position = lax.axis_index("tm")
    first = (position - reach) * hours
    row_ids = lax.broadcasted_iota(jnp.int32, (obs, rows), 1)
    obs_ids = lax.broadcasted_iota(jnp.int32, (obs, rows), 0)
    spread = ((row_ids >= obs_ids * bands) & (row_ids < (obs_ids + 1) * bands)).astype(F32).astype(BF16)
    ahead = hour_ref[...] - lag_ref[...] - first
    ahead = jnp.concatenate([ahead, jnp.zeros((8 - bands % 8, obs), jnp.int32)], axis=0) if bands % 8 else ahead
    ahead = jnp.dot(ahead.astype(F32).astype(BF16), spread, preferred_element_type=F32)
    ahead = jnp.sum(ahead * band_ref[...], axis=0, keepdims=True)
    on = jnp.dot(mask_ref[...].astype(F32).astype(BF16), spread, preferred_element_type=F32)
    ids = lax.broadcasted_iota(jnp.int32, (8, obs), 1).astype(F32) + 1.0
    ids = jnp.dot(ids.astype(BF16), spread, preferred_element_type=F32)[:1]
    valid = ahead >= (-first).astype(F32)
    members, lines = [], []
    for block in range(reach + 1):
        low = hours * (reach - block)
        member = (ahead >= low) & (ahead < low + hours) & valid
        members.append(member.astype(F32))
    head = jnp.concatenate(members + [jnp.zeros((8 - (reach + 1) % 8, rows), F32)], axis=0)
    lines = [head] + [members[block] * on for block in range(1, reach + 1)]
    before = lax.broadcasted_iota(jnp.int32, (rows, rows), 0) < lax.broadcasted_iota(jnp.int32, (rows, rows), 1)
    before = before.astype(F32).astype(BF16)
    ranks = jnp.dot(jnp.concatenate(lines, axis=0).astype(BF16), before, preferred_element_type=F32)
    over = jnp.zeros((1, rows), F32)
    pos = jnp.full((tiles, rows), -1.0, F32)
    tile_ids = lax.broadcasted_iota(jnp.int32, (tiles, rows), 0)
    odd = (tile_ids & 1) == 1
    halves = lax.broadcasted_iota(jnp.int32, (tiles, tiles), 0) >> 1
    halves = (halves == (lax.broadcasted_iota(jnp.int32, (tiles, tiles), 1) >> 1)).astype(F32).astype(BF16)
    crowded = jnp.zeros((tiles, 1), F32)
    base = caps[0]
    for block in range(reach + 1):
        member = members[block]
        rank = ranks[block : block + 1]
        over = jnp.maximum(over, jnp.where((member > 0) & (rank >= caps[block]), 1.0, 0.0))
        row_slot = jnp.where(member > 0, rank, -1.0)
        if block == 0:
            pos = jnp.where((member * on > 0) & (rank < caps[0]), rank, pos)
            order = jnp.zeros((tiles, rows), F32)
        else:
            start = head.shape[0] + (block - 1) * tiles
            tile_rank = ranks[start : start + tiles]
            inside = member * on > 0
            excess = jnp.where(inside & (tile_rank >= slots[block]), 1.0, 0.0)
            over = jnp.maximum(over, jnp.max(excess, axis=0, keepdims=True))
            both = jnp.dot(halves, inside.astype(F32).astype(BF16), preferred_element_type=F32)
            both = jnp.sum(both, axis=1, keepdims=True)
            crowded = jnp.maximum(crowded, jnp.where(both > pairs[block], 1.0, 0.0))
            place = jnp.where(odd, slots[block] - 1.0 - tile_rank, tile_rank)
            pos = jnp.where(inside & (tile_rank < slots[block]), place + base, pos)
            order = jnp.where(inside, place + 1.0, 0.0)
            base += slots[block]
        hour_of = lax.broadcasted_iota(jnp.int32, (hours, rows), 0).astype(F32) + float(hours * (reach - block))
        match = jnp.where((ahead == hour_of) & valid, 1.0, 0.0)
        tail = jnp.where(lax.broadcasted_iota(jnp.int32, (8, rows), 0) == 0, ids, 0.0)
        values = jnp.concatenate([order, match, tail], axis=0).astype(BF16)
        select = lax.broadcasted_iota(jnp.int32, (caps[block], rows), 0).astype(F32) == row_slot
        select = select.astype(F32).astype(BF16)
        meta_refs[block][...] = contract(values, select, 1, 1).astype(BF16)
    pos_ref[...] = pos
    over = jnp.maximum(jnp.max(over, axis=1, keepdims=True), jnp.max(crowded, axis=0, keepdims=True))
    flag_ref[...] = jnp.broadcast_to(over, (8, 128))


def prepare(caps, slots, pairs, hours, band_lag, obs_hour, tile_mask):
    obs, bands = band_lag.shape
    tiles = tile_mask.shape[1]
    rows = obs * bands
    pad = bands + (8 - bands % 8 if bands % 8 else 0)
    band = (jnp.arange(rows) % bands == jnp.arange(pad)[:, None]).astype(F32)
    vmem = pl.BlockSpec(memory_space=pltpu.VMEM)
    shapes = [
        jax.ShapeDtypeStruct((tiles, rows), F32),
        jax.ShapeDtypeStruct((8, 128), F32),
    ] + [jax.ShapeDtypeStruct((tiles + hours + 8, cap), BF16) for cap in caps]
    return pl.pallas_call(
        functools.partial(prep_kernel, caps, slots, pairs),
        in_specs=[vmem] * 4,
        out_specs=[vmem] * len(shapes),
        out_shape=shapes,
        compiler_params=pltpu.CompilerParams(vmem_limit_bytes=VMEM_LIMIT),
        name="prep",
    )(band_lag.T, obs_hour[None, :], tile_mask.T, band)


def split_dot(left, right, left_dim, right_dim):
    total = None
    for _ in range(3):
        term = left.astype(BF16)
        left = left - term.astype(F32)
        part = contract(term, right, left_dim, right_dim)
        total = part if total is None else total + part
    return total


def bulk_kernel(geometry, *refs):
    caps, slots, pairs, tiles, hours, axis = geometry
    reach = len(caps) - 1
    blocks = range(1, reach + 1)
    refs = list(refs)

    def take(count):
        head = refs[:count]
        del refs[:count]
        return head

    (prints_ref, flux_hbm, pos_ref, flag_ref, value_ref, weight_ref) = take(6)
    meta_refs = take(reach + 1)
    (dense_ref, modeled_ref, flag_out) = take(3)
    line_refs = take(reach + 1)
    match_refs = take(reach + 1)
    (prints_buf, flux_ref, local_buf, dense_buf, part_own, part_in, total_buf, other_buf,
     res_buf, res_in, flag_buf, flag_in) = take(12)
    send_refs, recv_refs, found_refs, got_refs, column_refs = (
        take(reach), take(reach), take(reach + 1), take(reach), take(reach))
    (relay_ref, relay_one) = take(2)
    (prints_sem, flux_sem, local_sem, dense_sem, send_sem, recv_sem, relay_in_sem, relay_out_sem,
     one_in_sem, one_out_sem, meta_send, meta_recv, part_send, part_recv, core_sem, res_send, res_recv,
     flag_sem) = take(18)

    me = lax.axis_index("tm")
    core = lax.axis_index("cells")
    obs = value_ref.shape[1]
    samples = value_ref.shape[0]
    groups = tiles // GROUP
    wide = GROUP * 128
    quad = lax.rem(me, 4)
    relays = axis % 4 == 0 and reach >= 2

    def to(tm):
        return {"tm": tm}

    partners = [step for step in (1, 2, 3, 4) if step < axis]
    hops = []
    step = 1
    while step < axis:
        hops.append(step)
        step *= 2
    far = [hop for hop in hops if hop > 4]

    def flip(hop):
        return jnp.where(lax.rem(me // hop, 2) == 0, me + hop, me - hop)

    barrier = pltpu.get_barrier_semaphore()
    count = jnp.int32(0)
    for step in partners:
        for target, exists in ((me + step, me + step < axis), (me - step, me >= step)):
            @pl.when(exists)
            def _():
                pl.semaphore_signal(barrier, inc=1, device_id=to(target), device_id_type=MESH)
            count = count + exists.astype(jnp.int32)
    for hop in far:
        pl.semaphore_signal(barrier, inc=1, device_id=to(flip(hop)), device_id_type=MESH)
        count = count + 1
    pl.semaphore_signal(barrier, inc=1, device_id={"cells": 1 - core}, device_id_type=MESH)
    count = count + 1

    def fetch(group, slot):
        return pltpu.make_async_copy(
            prints_ref.at[:, :, pl.ds(pl.multiple_of(group * wide, wide), wide)],
            prints_buf.at[slot], prints_sem.at[slot])

    fetch(0, 0).start()
    flux_copy = pltpu.make_async_copy(flux_hbm, flux_ref, flux_sem)
    flux_copy.start()
    pl.semaphore_wait(barrier, count)

    def remote(src, dst, ssem, rsem, target):
        return pltpu.make_async_remote_copy(
            src_ref=src, dst_ref=dst, send_sem=ssem, recv_sem=rsem,
            device_id=target, device_id_type=MESH)

    def meta_copy(block, target):
        return remote(meta_refs[block], got_refs[block - 1], meta_send.at[block - 1], meta_recv.at[block - 1], to(target))

    for block in blocks:
        @pl.when(me >= block)
        def _():
            meta_copy(block, me - block).start()

    def bulk_copy(block, group, source, target, dst=None, ssem=None, rsem=None):
        return remote(source, recv_refs[block - 1].at[group] if dst is None else dst,
                      send_sem.at[block - 1, group] if ssem is None else ssem,
                      recv_sem.at[block - 1, group] if rsem is None else rsem, to(target))

    def send(block, group):
        source = send_refs[block - 1].at[group]
        exists = me >= block
        detour = None
        if relays and block == 2:
            detour = (quad == 0) & (lax.rem(group, 4) != 2)
            copy = bulk_copy(2, group, source, me + 2, relay_ref.at[group], None, relay_in_sem.at[group])
        elif relays and block == 1:
            detour = (lax.rem(me, 2) == 0) & (lax.rem(group, 4) == 2)
            copy = bulk_copy(1, group, source, jnp.where(quad == 0, me + 2, me - 2),
                             relay_one.at[group // 4], None, one_in_sem.at[group // 4])
        if detour is None:
            @pl.when(exists)
            def _():
                bulk_copy(block, group, source, me - block).start()
        else:
            @pl.when(exists & detour)
            def _():
                copy.start()

            @pl.when(exists & jnp.logical_not(detour))
            def _():
                bulk_copy(block, group, source, me - block).start()

    def forward_two(group):
        return bulk_copy(2, group, relay_ref.at[group], me - 4, None, relay_out_sem.at[group])

    def forward_one(group):
        return bulk_copy(1, group, relay_one.at[group // 4], jnp.where(quad == 0, me + 1, me - 3),
                         None, one_out_sem.at[group // 4])

    is_two = (quad == 2) & (me >= 6)
    is_one = (lax.rem(me, 2) == 0) & (me != 2)
    def relay(group):
        if relays:
            @pl.when(is_two & (lax.rem(group, 4) != 2))
            def _():
                bulk_copy(2, group, send_refs[1].at[group], me - 4, relay_ref.at[group],
                          None, relay_in_sem.at[group]).wait_recv()
                forward_two(group).start()

            @pl.when(is_one & (lax.rem(group, 4) == 2))
            def _():
                bulk_copy(1, group, send_refs[0].at[group], me, relay_one.at[group // 4],
                          None, one_in_sem.at[group // 4]).wait_recv()
                forward_one(group).start()

    def launch(group):
        for block in blocks:
            send(block, group)

    for block in blocks:
        @pl.when(me + block >= axis)
        def _():
            recv_refs[block - 1][...] = jnp.zeros_like(recv_refs[block - 1])
            got_refs[block - 1][...] = jnp.zeros_like(got_refs[block - 1])
    flag_buf[0] = flag_ref[...]
    for found in found_refs:
        found[...] = jnp.zeros_like(found)
    flux_copy.wait()

    total_slots = caps[0] + sum(slots[1:])
    starts = [0, caps[0]]
    for block in blocks:
        starts.append(starts[-1] + slots[block])
    bases = [sum(caps[:block]) for block in range(reach + 1)]

    def columns(group):
        return pl.ds(pl.multiple_of(group * wide, wide), wide)

    def local_out(group, slot):
        return pltpu.make_async_copy(local_buf.at[slot], dense_ref.at[pl.ds(0, caps[0]), columns(group)], local_sem.at[slot])

    def dense_out(group, slot):
        return pltpu.make_async_copy(
            dense_buf.at[slot], dense_ref.at[pl.ds(caps[0], sum(caps[1:])), columns(group)], dense_sem.at[slot])

    def accumulate(block, group, rows):
        found_refs[block][...] += contract(flux_ref[:, columns(group)], rows, 1, 1)

    def pack(group):
        slot = lax.rem(group, 2)
        fetch(group, slot).wait()

        @pl.when(group + 1 < groups)
        def _():
            fetch(group + 1, 1 - slot).start()

        @pl.when(group >= 2)
        def _():
            local_out(group - 2, slot).wait()

        @pl.when(group >= 1)
        def _():
            launch(group - 1)

        prints = prints_buf[slot].reshape(prints_buf.shape[1] * prints_buf.shape[2], wide)
        slot_ids = lax.broadcasted_iota(jnp.int32, (total_slots, 1), 0).astype(F32)
        ends = []
        for half in range(GROUP):
            tile = group * GROUP + half
            select = (slot_ids == pos_ref[pl.ds(tile, 1), :]).astype(F32).astype(BF16)
            packed = jnp.dot(select, prints[:, half * 128 : (half + 1) * 128], preferred_element_type=F32).astype(BF16)
            local_buf[slot, :, half * 128 : (half + 1) * 128] = packed[: caps[0]]
            ends.append(packed)
        for block in blocks:
            first, last = (packed[starts[block] : starts[block + 1]] for packed in ends)
            gap, window = pairs[block] - slots[block], slots[block]
            send_refs[block - 1][group, :gap] = first[:gap]
            if window > gap:
                send_refs[block - 1][group, gap:window] = first[gap:] + last[: window - gap]
            send_refs[block - 1][group, window:] = last[window - gap :]
        local_out(group, slot).start()
        accumulate(0, group, local_buf[slot])

    def receive_tables():
        for block in blocks:
            @pl.when(me + block < axis)
            def _():
                meta_copy(block, me).wait_recv()
            meta = got_refs[block - 1][...].astype(F32)
            top = meta[:tiles]
            top = jnp.concatenate([top, jnp.zeros((128 - tiles, top.shape[1]), F32)], axis=0)
            column_refs[block - 1][...] = top.T.astype(BF16)


    def unpack(group):
        slot = lax.rem(group, 2)

        def flag_copy(index):
            target = {"cells": 1 - core} if index == len(hops) else to(flip(hops[index]))
            return remote(flag_buf.at[index], flag_in.at[index], flag_sem.at[0, index], flag_sem.at[1, index], target)

        for index in range(len(hops) + 1):
            @pl.when(group == 2 * index)
            def _():
                flag_copy(index).start()

            @pl.when(group == 2 * index + 1)
            def _():
                flag_copy(index).wait()
                merged = jnp.maximum(flag_buf[index], flag_in[index])
                flag_buf[index + 1] = merged

        @pl.when(group >= 2)
        def _():
            dense_out(group - 2, slot).wait()

        for block in blocks:
            @pl.when(me + block < axis)
            def _():
                bulk_copy(block, group, send_refs[block - 1].at[group], me).wait_recv()
            low = bases[block] - caps[0]
            for half in range(GROUP):
                tile = group * GROUP + half
                pick = lax.broadcasted_iota(jnp.int32, (128, slots[block]), 0) == tile
                spread = jnp.dot(column_refs[block - 1][...], pick.astype(F32).astype(BF16), preferred_element_type=F32)
                ids = lax.broadcasted_iota(jnp.int32, (1, slots[block]), 1).astype(F32) + 1.0
                place = (spread == ids).astype(F32).astype(BF16)
                start = half * (pairs[block] - slots[block])
                window = recv_refs[block - 1][group, start : start + slots[block]]
                rows = jnp.dot(place, window, preferred_element_type=F32).astype(BF16)
                dense_buf[slot, low : low + caps[block], half * 128 : (half + 1) * 128] = rows
            accumulate(block, group, dense_buf[slot, low : low + caps[block], :])
        dense_out(group, slot).start()

    def step_through(index, carry):
        @pl.when(index < groups)
        def _():
            pack(index)

        @pl.when(index == groups)
        def _():
            launch(groups - 1)

        @pl.when((index >= RELAY_LAG) & (index < groups + RELAY_LAG))
        def _():
            relay(index - RELAY_LAG)

        @pl.when(index == UNPACK_LAG)
        def _():
            receive_tables()

        @pl.when(index >= UNPACK_LAG)
        def _():
            unpack(index - UNPACK_LAG)
        return carry

    lax.fori_loop(0, groups + UNPACK_LAG, step_through, 0)
    for group in range(max(0, groups - 2), groups):
        local_out(group, group % 2).wait()
    for group in range(max(0, groups - 2), groups):
        dense_out(group, group % 2).wait()
    flag_out[...] = flag_buf[len(hops) + 1][:1, :1]

    def table(block):
        return meta_refs[0] if block == 0 else got_refs[block - 1]

    def owners(block):
        ids = table(block)[tiles + hours : tiles + hours + 8, :].astype(F32)[:1]
        rows = lax.broadcasted_iota(jnp.int32, (obs, caps[block]), 0).astype(F32) + 1.0
        return (rows == ids).astype(F32).astype(BF16)

    def partial_of(block):
        match = table(block)[tiles : tiles + hours, :].astype(F32)
        found = found_refs[block][...].reshape(samples, hours, caps[block])
        return split_dot(jnp.sum(found * match[None], axis=1), owners(block), 1, 1)

    def part_copy(block, target):
        return remote(part_own.at[block - 1], part_in.at[block - 1], part_send.at[block - 1], part_recv.at[block - 1], to(target))

    def part_start(block):
        @pl.when(me + block < axis)
        def _():
            part_copy(block, me + block).start()

    for block in blocks:
        @pl.when(me < block)
        def _():
            part_in[block - 1] = jnp.zeros((samples, obs), F32)
    for block in reversed(blocks):
        part_own[block - 1] = partial_of(block)
        if block < reach:
            part_start(block + 1)
    total = partial_of(0)
    part_start(1)
    for block in blocks:
        @pl.when(me >= block)
        def _():
            part_copy(block, me).wait_recv()
        total = total + part_in[block - 1]
    total_buf[...] = total
    swap = remote(total_buf, other_buf, core_sem.at[0], core_sem.at[1], {"cells": 1 - core})
    swap.start()
    swap.wait()
    modeled = total_buf[...] + other_buf[...]
    modeled_ref[...] = modeled
    residual = (weight_ref[...] * (modeled - value_ref[...])).astype(BF16)
    res_buf[...] = residual

    def res_copy(block, target):
        return remote(res_buf, res_in.at[block - 1], res_send.at[block - 1], res_recv.at[block - 1], to(target))

    line_refs[0][...] = contract(residual, owners(0), 1, 0).astype(BF16)
    for block in reversed(blocks):
        @pl.when(me >= block)
        def _():
            res_copy(block, me - block).start()

        @pl.when(me + block >= axis)
        def _():
            res_in[block - 1] = jnp.zeros((samples, obs), BF16)
    for block in range(reach + 1):
        match_refs[block][...] = table(block)[tiles : tiles + hours, :]
    for block in blocks:
        @pl.when(me + block < axis)
        def _():
            res_copy(block, me).wait_recv()
        line_refs[block][...] = contract(res_in[block - 1], owners(block), 1, 0).astype(BF16)

    for block in blocks:
        @pl.when(me >= block)
        def _():
            meta_copy(block, me).wait_send()
            res_copy(block, me).wait_send()

        @pl.when(me + block < axis)
        def _():
            part_copy(block, me).wait_send()

    def drain(group, carry):
        for block in blocks:
            @pl.when(me >= block)
            def _():
                bulk_copy(block, group, send_refs[block - 1].at[group], me).wait_send()
        if relays:
            @pl.when(is_two & (lax.rem(group, 4) != 2))
            def _():
                forward_two(group).wait_send()

            @pl.when(is_one & (lax.rem(group, 4) == 2))
            def _():
                forward_one(group).wait_send()
        return carry

    lax.fori_loop(0, groups, drain, 0)


def exchange(caps, slots, pairs, flux, footprint, pos, flag, metas, obs_value, obs_weight, axis):
    samples, hours, cells = flux.shape
    obs, bands, _ = footprint.shape
    tiles = pos.shape[0]
    reach = len(caps) - 1
    groups = tiles // GROUP
    wide = GROUP * 128
    lines = samples * hours
    hop_count = max(1, math.ceil(math.log2(axis)))
    vmem = pl.BlockSpec(memory_space=pltpu.VMEM)
    anywhere = pl.BlockSpec(memory_space=pl.ANY)
    dma = pltpu.SemaphoreType.DMA
    depth = sum(caps)
    out_shape = [
        jax.ShapeDtypeStruct((depth, cells), BF16),
        jax.ShapeDtypeStruct((samples, obs), F32),
        jax.ShapeDtypeStruct((1, 1), F32),
    ]
    out_shape += [jax.ShapeDtypeStruct((samples, cap), BF16) for cap in caps]
    out_shape += [jax.ShapeDtypeStruct((hours, cap), BF16) for cap in caps]
    scratch = [
        pltpu.VMEM((2, obs, bands, wide), BF16),
        pltpu.VMEM((lines, cells), BF16),
        pltpu.VMEM((2, caps[0], wide), BF16),
        pltpu.VMEM((2, depth - caps[0], wide), BF16),
        pltpu.VMEM((reach, samples, obs), F32),
        pltpu.VMEM((reach, samples, obs), F32),
        pltpu.VMEM((samples, obs), F32),
        pltpu.VMEM((samples, obs), F32),
        pltpu.VMEM((samples, obs), BF16),
        pltpu.VMEM((reach, samples, obs), BF16),
        pltpu.VMEM((hop_count + 2, 8, 128), F32),
        pltpu.VMEM((hop_count + 1, 8, 128), F32),
    ]
    scratch += [pltpu.VMEM((groups, pair, 128), BF16) for pair in pairs[1:]] * 2
    scratch += [pltpu.VMEM((lines, cap), F32) for cap in caps]
    scratch += [pltpu.VMEM(metas[0].shape[:1] + (cap,), BF16) for cap in caps[1:]]
    scratch += [pltpu.VMEM((cap, 128), BF16) for cap in caps[1:]]
    scratch += [
        pltpu.VMEM((groups, pairs[min(2, reach)], 128), BF16),
        pltpu.VMEM((max(1, groups // 4), pairs[1], 128), BF16),
    ]
    scratch += [
        dma((2,)), dma, dma((2,)), dma((2,)),
        dma((reach, groups)), dma((reach, groups)),
        dma((groups,)), dma((groups,)), dma((max(1, groups // 4),)), dma((max(1, groups // 4),)),
        dma((reach,)), dma((reach,)), dma((reach,)), dma((reach,)),
        dma((2,)), dma((reach,)), dma((reach,)), dma((2, hop_count + 1)),
    ]
    geometry = (caps, slots, pairs, tiles, hours, axis)
    return pl.pallas_call(
        functools.partial(bulk_kernel, geometry),
        in_specs=[anywhere, anywhere] + [vmem] * (4 + len(metas)),
        out_specs=[anywhere] + [vmem] * (len(out_shape) - 1),
        out_shape=out_shape,
        scratch_shapes=scratch,
        compiler_params=pltpu.CompilerParams(
            collective_id=0, has_side_effects=True, vmem_limit_bytes=VMEM_LIMIT),
        name="bulk",
    )(footprint, flux.reshape(lines, cells), pos, flag, obs_value, obs_weight[None, :], *metas)


def adjoint_kernel(count, *refs):
    dense_ref, out_ref, line_buf = refs[2 * count], refs[2 * count + 1], refs[2 * count + 2]

    @pl.when(pl.program_id(0) == 0)
    def _():
        pieces = []
        for line, match in zip(refs[:count], refs[count : 2 * count]):
            values = line[...].astype(F32)[:, None, :] * match[...].astype(F32)[None]
            pieces.append(values.reshape(-1, values.shape[2]))
        line_buf[...] = jnp.concatenate(pieces, axis=1).astype(BF16)

    out_ref[...] = jnp.dot(line_buf[...], dense_ref[...], preferred_element_type=F32)


def adjoint(lines, matches, dense):
    depth, cells = dense.shape
    tile = min(TILE_CELLS, cells)
    height = lines[0].shape[0] * matches[0].shape[0]
    whole = [pl.BlockSpec(part.shape, lambda i: (0, 0)) for part in lines + matches]
    return pl.pallas_call(
        functools.partial(adjoint_kernel, len(lines)),
        grid=(cells // tile,),
        in_specs=whole + [pl.BlockSpec((depth, tile), lambda i: (0, i))],
        out_specs=pl.BlockSpec((height, tile), lambda i: (0, i)),
        out_shape=jax.ShapeDtypeStruct((height, cells), F32),
        scratch_shapes=[pltpu.VMEM((height, depth), BF16)],
        compiler_params=pltpu.CompilerParams(
            dimension_semantics=("arbitrary",), vmem_limit_bytes=VMEM_LIMIT),
        name="adjoint",
    )(*lines, *matches, dense)


def whole_plan(reach, flux, footprint, band_lag, obs_hour, tile_mask, obs_value, obs_weight):
    samples, hours, cells = flux.shape
    obs, bands, _ = footprint.shape
    rows = obs * bands
    position = lax.axis_index("tm")
    tiles = tile_mask.shape[1]
    source = (obs_hour[:, None] - band_lag).reshape(1, rows)
    hour_ids = lax.broadcasted_iota(jnp.int32, (hours, rows), 0)
    obs_ids = lax.broadcasted_iota(jnp.int32, (rows, obs), 0) // bands
    owner = (obs_ids == lax.broadcasted_iota(jnp.int32, (rows, obs), 1)).astype(BF16)
    masked = footprint.reshape(obs, bands, tiles, cells // tiles) * tile_mask.astype(BF16)[:, None, :, None]
    masked = masked.reshape(rows, cells)
    flux_lines = flux.reshape(samples * hours, cells)
    blocks = range(reach + 1)

    def sent(value, steps):
        return shifted(value, "tm", steps) if steps else value

    prints, matches = [], []
    for block in blocks:
        match = ((source == hour_ids + (position - block) * hours) & (source >= 0)).astype(BF16)
        prints.append(sent(masked, -block))
        matches.append(sent(match, -block))
    prints, matches = jnp.stack(prints), jnp.stack(matches)

    def forward(pair):
        found = contract(flux_lines, pair[0], 1, 1).reshape(samples, hours, rows)
        return jnp.sum(found * pair[1].astype(F32)[None], axis=1)

    found = lax.map(forward, (prints, matches))
    total = sum(sent(found[block], block) for block in blocks)
    total = contract(total, owner.astype(F32), 1, 0, precision=lax.Precision.HIGHEST)
    modeled = over_axis(total, "cells")
    residual = (obs_weight[None, :] * (modeled - obs_value)).astype(BF16)
    values = contract(residual, owner, 1, 1, BF16)
    values = jnp.stack([sent(values, -block) for block in blocks])

    def backward(gradient, parts):
        lines = (parts[0][:, None, :] * parts[1][None]).reshape(samples * hours, rows)
        return gradient + contract(lines, parts[2], 1, 0), None

    gradient = jnp.zeros((samples * hours, cells), F32)
    gradient, _ = lax.scan(backward, gradient, (values, matches, prints))
    return modeled, gradient


def body(axis, flux, footprint, band_lag, obs_hour, tile_mask, obs_value, obs_weight):
    samples, hours, cells = flux.shape
    obs, bands, _ = footprint.shape
    tiles = tile_mask.shape[1]
    reach = -(-(LAGS - 1) // hours)
    sizes = [capacities(block, hours, obs, bands) for block in range(reach + 1)]
    caps = tuple(size[0] for size in sizes)
    slots = tuple(size[1] for size in sizes)
    pairs = tuple(size[2] for size in sizes)
    pos, flag, *metas = prepare(caps, slots, pairs, hours, band_lag, obs_hour, tile_mask)
    outs = exchange(caps, slots, pairs, flux, footprint, pos, flag, metas, obs_value, obs_weight, axis)
    dense, modeled, flags = outs[:3]
    lines = list(outs[3 : 4 + reach])
    matches = list(outs[4 + reach :])

    def slow():
        return whole_plan(reach, flux, footprint, band_lag, obs_hour, tile_mask, obs_value, obs_weight)

    def fast():
        return modeled, adjoint(lines, matches, dense)

    modeled, gradient = lax.cond(flags[0, 0] > 0, slow, fast)
    return modeled, gradient.reshape(samples, hours, cells)


def solution(mesh):
    placed = (
        P(None, "tm", "cells"),
        P("tm", None, "cells"),
        P("tm", None),
        P("tm"),
        P("tm", "cells"),
        P(None, "tm"),
        P("tm"),
    )
    return jax.shard_map(
        functools.partial(body, mesh.shape["tm"]),
        mesh=mesh,
        in_specs=placed,
        out_specs=(P(None, "tm"), P(None, "tm", "cells")),
        check_vma=False,
    )
```

```python
import functools
import math

import jax
import jax.numpy as jnp
import numpy as np
from jax import lax
from jax.experimental import pallas as pl
from jax.experimental.pallas import tpu as pltpu
from jax.sharding import PartitionSpec as P

LAGS = 24
GRAIN = 16
GROUP = 2
UNPACK_LAG = 4
RELAY_LAG = 3
TILE_CELLS = 1024
VMEM_LIMIT = 62 * 2**20
MESH = pl.DeviceIdType.MESH
BF16 = jnp.bfloat16
F32 = jnp.float32


def shifted(value, axis, steps):
    count = lax.axis_size(axis)
    initial, last = (max(0, -steps), min(count, count - steps))
    return lax.ppermute(value, axis, [(source, source + steps) for source in range(initial, last)])


def over_axis(value, axis):
    if lax.axis_size(axis) == 2:
        return value + lax.ppermute(value, axis, [(0, 1), (1, 0)])
    return lax.psum(value, axis)


def contract(left, right, left_dim, right_dim, out=F32, precision=None):
    return lax.dot_general(
        left, right, (((left_dim,), (right_dim,)), ((), ())),
        precision=precision, preferred_element_type=out,
    )


def capacities(block, hours, obs, bands):
    mean = spread = mean_square = 0.0
    for hour in range(hours):
        hits = sum(1 for lag in range(LAGS) if (hour - lag) // hours == -block)
        share = hits / LAGS
        mean += bands * share / hours
        mean_square += (bands * share) ** 2 / hours
        spread += bands * share * (1 - share) * (LAGS - bands) / (LAGS - 1) / hours
    spread += mean_square - mean**2
    rows = obs * mean + 4.0 * math.sqrt(obs * spread)
    half_spread = 0.5 * (spread + mean**2) - 0.25 * mean**2
    slots = 0.5 * obs * mean + 4.7 * math.sqrt(obs * half_spread)
    pair_spread = 1.5 * (spread + mean**2) - mean**2
    pairs = obs * mean + 4.65 * math.sqrt(obs * pair_spread)
    rows = min(obs * bands, GRAIN * math.ceil(rows / GRAIN))
    slots = min(rows, GRAIN * math.ceil(slots / GRAIN))
    return rows, slots, max(slots, min(2 * slots, GRAIN * math.ceil(pairs / GRAIN)))


def prep_kernel(caps, slots, pairs, lag_ref, hour_ref, mask_ref, band_ref, pos_ref, flag_ref, *meta_refs):
    reach = len(caps) - 1
    bands, obs = lag_ref.shape
    tiles = mask_ref.shape[0]
    rows = bands * obs
    hours = meta_refs[0].shape[0] - tiles - 8
    position = lax.axis_index("tm")
    first = (position - reach) * hours
    row_ids = lax.broadcasted_iota(jnp.int32, (obs, rows), 1)
    obs_ids = lax.broadcasted_iota(jnp.int32, (obs, rows), 0)
    spread = ((row_ids >= obs_ids * bands) & (row_ids < (obs_ids + 1) * bands)).astype(F32).astype(BF16)
    ahead = hour_ref[...] - lag_ref[...] - first
    ahead = jnp.concatenate([ahead, jnp.zeros((8 - bands % 8, obs), jnp.int32)], axis=0) if bands % 8 else ahead
    ahead = jnp.dot(ahead.astype(F32).astype(BF16), spread, preferred_element_type=F32)
    ahead = jnp.sum(ahead * band_ref[...], axis=0, keepdims=True)
    on = jnp.dot(mask_ref[...].astype(F32).astype(BF16), spread, preferred_element_type=F32)
    ids = lax.broadcasted_iota(jnp.int32, (8, obs), 1).astype(F32) + 1.0
    ids = jnp.dot(ids.astype(BF16), spread, preferred_element_type=F32)[:1]
    valid = ahead >= (-first).astype(F32)
    members, lines = [], []
    for block in range(reach + 1):
        low = hours * (reach - block)
        member = (ahead >= low) & (ahead < low + hours) & valid
        members.append(member.astype(F32))
    head = jnp.concatenate(members + [jnp.zeros((8 - (reach + 1) % 8, rows), F32)], axis=0)
    lines = [head] + [members[block] * on for block in range(1, reach + 1)]
    before = lax.broadcasted_iota(jnp.int32, (rows, rows), 0) < lax.broadcasted_iota(jnp.int32, (rows, rows), 1)
    before = before.astype(F32).astype(BF16)
    ranks = jnp.dot(jnp.concatenate(lines, axis=0).astype(BF16), before, preferred_element_type=F32)
    over = jnp.zeros((1, rows), F32)
    pos = jnp.full((tiles, rows), -1.0, F32)
    tile_ids = lax.broadcasted_iota(jnp.int32, (tiles, rows), 0)
    odd = (tile_ids & 1) == 1
    halves = lax.broadcasted_iota(jnp.int32, (tiles, tiles), 0) >> 1
    halves = (halves == (lax.broadcasted_iota(jnp.int32, (tiles, tiles), 1) >> 1)).astype(F32).astype(BF16)
    crowded = jnp.zeros((tiles, 1), F32)
    base = caps[0]
    for block in range(reach + 1):
        member = members[block]
        rank = ranks[block : block + 1]
        over = jnp.maximum(over, jnp.where((member > 0) & (rank >= caps[block]), 1.0, 0.0))
        row_slot = jnp.where(member > 0, rank, -1.0)
        if block == 0:
            pos = jnp.where((member * on > 0) & (rank < caps[0]), rank, pos)
            order = jnp.zeros((tiles, rows), F32)
        else:
            start = head.shape[0] + (block - 1) * tiles
            tile_rank = ranks[start : start + tiles]
            inside = member * on > 0
            excess = jnp.where(inside & (tile_rank >= slots[block]), 1.0, 0.0)
            over = jnp.maximum(over, jnp.max(excess, axis=0, keepdims=True))
            both = jnp.dot(halves, inside.astype(F32).astype(BF16), preferred_element_type=F32)
            both = jnp.sum(both, axis=1, keepdims=True)
            crowded = jnp.maximum(crowded, jnp.where(both > pairs[block], 1.0, 0.0))
            place = jnp.where(odd, slots[block] - 1.0 - tile_rank, tile_rank)
            pos = jnp.where(inside & (tile_rank < slots[block]), place + base, pos)
            order = jnp.where(inside, place + 1.0, 0.0)
            base += slots[block]
        hour_of = lax.broadcasted_iota(jnp.int32, (hours, rows), 0).astype(F32) + float(hours * (reach - block))
        match = jnp.where((ahead == hour_of) & valid, 1.0, 0.0)
        tail = jnp.where(lax.broadcasted_iota(jnp.int32, (8, rows), 0) == 0, ids, 0.0)
        values = jnp.concatenate([order, match, tail], axis=0).astype(BF16)
        select = lax.broadcasted_iota(jnp.int32, (caps[block], rows), 0).astype(F32) == row_slot
        select = select.astype(F32).astype(BF16)
        meta_refs[block][...] = contract(values, select, 1, 1).astype(BF16)
    pos_ref[...] = pos
    over = jnp.maximum(jnp.max(over, axis=1, keepdims=True), jnp.max(crowded, axis=0, keepdims=True))
    flag_ref[...] = jnp.broadcast_to(over, (8, 128))


def prepare(caps, slots, pairs, hours, band_lag, obs_hour, tile_mask):
    obs, bands = band_lag.shape
    tiles = tile_mask.shape[1]
    rows = obs * bands
    pad = bands + (8 - bands % 8 if bands % 8 else 0)
    band = np.equal(np.arange(rows) % bands, np.arange(pad)[:, None]).astype(np.float32)
    vmem = pl.BlockSpec(memory_space=pltpu.VMEM)
    shapes = [
        jax.ShapeDtypeStruct((tiles, rows), F32),
        jax.ShapeDtypeStruct((8, 128), F32),
    ] + [jax.ShapeDtypeStruct((tiles + hours + 8, cap), BF16) for cap in caps]
    return pl.pallas_call(
        functools.partial(prep_kernel, caps, slots, pairs),
        in_specs=[vmem] * 4,
        out_specs=[vmem] * len(shapes),
        out_shape=shapes,
        compiler_params=pltpu.CompilerParams(vmem_limit_bytes=VMEM_LIMIT),
        name="prep",
    )(band_lag.T, obs_hour[None, :], tile_mask.T, band)


def split_dot(left, right, left_dim, right_dim):
    total = None
    for _ in range(3):
        term = left.astype(BF16)
        left = left - term.astype(F32)
        part = contract(term, right, left_dim, right_dim)
        total = part if total is None else total + part
    return total


def bulk_kernel(geometry, *refs):
    caps, slots, pairs, tiles, hours, axis = geometry
    reach = len(caps) - 1
    blocks = range(1, reach + 1)
    refs = list(refs)

    def take(count):
        head = refs[:count]
        del refs[:count]
        return head

    (prints_ref, flux_hbm, pos_ref, flag_ref, value_ref, weight_ref) = take(6)
    meta_refs = take(reach + 1)
    (dense_ref, modeled_ref, flag_out) = take(3)
    line_refs = take(reach + 1)
    match_refs = take(reach + 1)
    (prints_buf, flux_ref, local_buf, dense_buf, part_own, part_in, total_buf, other_buf,
     res_buf, res_in, flag_buf, flag_in) = take(12)
    send_refs, recv_refs, found_refs, got_refs, column_refs = (
        take(reach), take(reach), take(reach + 1), take(reach), take(reach))
    (relay_ref, relay_one) = take(2)
    (prints_sem, flux_sem, local_sem, dense_sem, send_sem, recv_sem, relay_in_sem, relay_out_sem,
     one_in_sem, one_out_sem, meta_send, meta_recv, part_send, part_recv, core_sem, res_send, res_recv,
     flag_sem) = take(18)

    me = lax.axis_index("tm")
    core = lax.axis_index("cells")
    obs = value_ref.shape[1]
    samples = value_ref.shape[0]
    groups = tiles // GROUP
    wide = GROUP * 128
    quad = lax.rem(me, 4)
    relays = axis % 4 == 0 and reach >= 2

    def to(tm):
        return {"tm": tm}

    partners = [step for step in (1, 2, 3, 4) if step < axis]
    hops = []
    step = 1
    while step < axis:
        hops.append(step)
        step *= 2
    far = [hop for hop in hops if hop > 4]

    def flip(hop):
        return jnp.where(lax.rem(me // hop, 2) == 0, me + hop, me - hop)

    barrier = pltpu.get_barrier_semaphore()
    count = jnp.int32(0)
    for step in partners:
        for target, exists in ((me + step, me + step < axis), (me - step, me >= step)):
            @pl.when(exists)
            def _():
                pl.semaphore_signal(barrier, inc=1, device_id=to(target), device_id_type=MESH)
            count = count + exists.astype(jnp.int32)
    for hop in far:
        pl.semaphore_signal(barrier, inc=1, device_id=to(flip(hop)), device_id_type=MESH)
        count = count + 1
    pl.semaphore_signal(barrier, inc=1, device_id={"cells": 1 - core}, device_id_type=MESH)
    count = count + 1

    def fetch(group, slot):
        return pltpu.make_async_copy(
            prints_ref.at[:, :, pl.ds(pl.multiple_of(group * wide, wide), wide)],
            prints_buf.at[slot], prints_sem.at[slot])

    fetch(0, 0).start()
    flux_copy = pltpu.make_async_copy(flux_hbm, flux_ref, flux_sem)
    flux_copy.start()
    pl.semaphore_wait(barrier, count)

    def remote(src, dst, ssem, rsem, target):
        return pltpu.make_async_remote_copy(
            src_ref=src, dst_ref=dst, send_sem=ssem, recv_sem=rsem,
            device_id=target, device_id_type=MESH)

    def meta_copy(block, target):
        return remote(meta_refs[block], got_refs[block - 1], meta_send.at[block - 1], meta_recv.at[block - 1], to(target))

    for block in blocks:
        @pl.when(me >= block)
        def _():
            meta_copy(block, me - block).start()

    def bulk_copy(block, group, source, target, dst=None, ssem=None, rsem=None):
        return remote(source, recv_refs[block - 1].at[group] if dst is None else dst,
                      send_sem.at[block - 1, group] if ssem is None else ssem,
                      recv_sem.at[block - 1, group] if rsem is None else rsem, to(target))

    def send(block, group):
        source = send_refs[block - 1].at[group]
        exists = me >= block
        detour = None
        if relays and block == 2:
            detour = (quad == 0) & (lax.rem(group, 4) != 2)
            copy = bulk_copy(2, group, source, me + 2, relay_ref.at[group], None, relay_in_sem.at[group])
        elif relays and block == 1:
            detour = (lax.rem(me, 2) == 0) & (lax.rem(group, 4) == 2)
            copy = bulk_copy(1, group, source, jnp.where(quad == 0, me + 2, me - 2),
                             relay_one.at[group // 4], None, one_in_sem.at[group // 4])
        if detour is None:
            @pl.when(exists)
            def _():
                bulk_copy(block, group, source, me - block).start()
        else:
            @pl.when(exists & detour)
            def _():
                copy.start()

            @pl.when(exists & jnp.logical_not(detour))
            def _():
                bulk_copy(block, group, source, me - block).start()

    def forward_two(group):
        return bulk_copy(2, group, relay_ref.at[group], me - 4, None, relay_out_sem.at[group])

    def forward_one(group):
        return bulk_copy(1, group, relay_one.at[group // 4], jnp.where(quad == 0, me + 1, me - 3),
                         None, one_out_sem.at[group // 4])

    is_two = (quad == 2) & (me >= 6)
    is_one = (lax.rem(me, 2) == 0) & (me != 2)
    def relay(group):
        if relays:
            @pl.when(is_two & (lax.rem(group, 4) != 2))
            def _():
                bulk_copy(2, group, send_refs[1].at[group], me - 4, relay_ref.at[group],
                          None, relay_in_sem.at[group]).wait_recv()
                forward_two(group).start()

            @pl.when(is_one & (lax.rem(group, 4) == 2))
            def _():
                bulk_copy(1, group, send_refs[0].at[group], me, relay_one.at[group // 4],
                          None, one_in_sem.at[group // 4]).wait_recv()
                forward_one(group).start()

    def launch(group):
        for block in [2, 1] + list(blocks)[2:] if reach >= 2 else blocks:
            send(block, group)

    for block in blocks:
        @pl.when(me + block >= axis)
        def _():
            recv_refs[block - 1][...] = jnp.zeros_like(recv_refs[block - 1])
            got_refs[block - 1][...] = jnp.zeros_like(got_refs[block - 1])
    flag_buf[0] = flag_ref[...]
    for found in found_refs:
        found[...] = jnp.zeros_like(found)
    flux_copy.wait()

    total_slots = caps[0] + sum(slots[1:])
    starts = [0, caps[0]]
    for block in blocks:
        starts.append(starts[-1] + slots[block])
    bases = [sum(caps[:block]) for block in range(reach + 1)]

    def columns(group):
        return pl.ds(pl.multiple_of(group * wide, wide), wide)

    def local_out(group, slot):
        return pltpu.make_async_copy(local_buf.at[slot], dense_ref.at[pl.ds(0, caps[0]), columns(group)], local_sem.at[slot])

    def dense_out(group, slot):
        return pltpu.make_async_copy(
            dense_buf.at[slot], dense_ref.at[pl.ds(caps[0], sum(caps[1:])), columns(group)], dense_sem.at[slot])

    def accumulate(block, group, rows):
        found_refs[block][...] += contract(flux_ref[:, columns(group)], rows, 1, 1)

    def pack(group):
        slot = lax.rem(group, 2)
        fetch(group, slot).wait()

        @pl.when(group + 1 < groups)
        def _():
            fetch(group + 1, 1 - slot).start()

        @pl.when(group >= 2)
        def _():
            local_out(group - 2, slot).wait()

        @pl.when(group >= 1)
        def _():
            launch(group - 1)

        prints = prints_buf[slot].reshape(prints_buf.shape[1] * prints_buf.shape[2], wide)
        slot_ids = lax.broadcasted_iota(jnp.int32, (total_slots, 1), 0).astype(F32)
        ends = []
        for half in range(GROUP):
            tile = group * GROUP + half
            select = (slot_ids == pos_ref[pl.ds(tile, 1), :]).astype(F32).astype(BF16)
            packed = jnp.dot(select, prints[:, half * 128 : (half + 1) * 128], preferred_element_type=F32).astype(BF16)
            local_buf[slot, :, half * 128 : (half + 1) * 128] = packed[: caps[0]]
            ends.append(packed)
        for block in blocks:
            first, last = (packed[starts[block] : starts[block + 1]] for packed in ends)
            gap, window = pairs[block] - slots[block], slots[block]
            send_refs[block - 1][group, :gap] = first[:gap]
            if window > gap:
                send_refs[block - 1][group, gap:window] = first[gap:] + last[: window - gap]
            send_refs[block - 1][group, window:] = last[window - gap :]
        local_out(group, slot).start()
        accumulate(0, group, local_buf[slot])

    def receive_tables():
        for block in blocks:
            @pl.when(me + block < axis)
            def _():
                meta_copy(block, me).wait_recv()
            meta = got_refs[block - 1][...].astype(F32)
            top = meta[:tiles]
            top = jnp.concatenate([top, jnp.zeros((128 - tiles, top.shape[1]), F32)], axis=0)
            column_refs[block - 1][...] = top.T.astype(BF16)


    def unpack(group):
        slot = lax.rem(group, 2)

        def flag_copy(index):
            target = {"cells": 1 - core} if index == len(hops) else to(flip(hops[index]))
            return remote(flag_buf.at[index], flag_in.at[index], flag_sem.at[0, index], flag_sem.at[1, index], target)

        for index in range(len(hops) + 1):
            @pl.when(group == 2 * index)
            def _():
                flag_copy(index).start()

            @pl.when(group == 2 * index + 1)
            def _():
                flag_copy(index).wait()
                merged = jnp.maximum(flag_buf[index], flag_in[index])
                flag_buf[index + 1] = merged

        @pl.when(group >= 2)
        def _():
            dense_out(group - 2, slot).wait()

        for block in blocks:
            @pl.when(me + block < axis)
            def _():
                bulk_copy(block, group, send_refs[block - 1].at[group], me).wait_recv()
            low = bases[block] - caps[0]
            for half in range(GROUP):
                tile = group * GROUP + half
                pick = lax.broadcasted_iota(jnp.int32, (128, slots[block]), 0) == tile
                spread = jnp.dot(column_refs[block - 1][...], pick.astype(F32).astype(BF16), preferred_element_type=F32)
                ids = lax.broadcasted_iota(jnp.int32, (1, slots[block]), 1).astype(F32) + 1.0
                place = (spread == ids).astype(F32).astype(BF16)
                start = half * (pairs[block] - slots[block])
                window = recv_refs[block - 1][group, start : start + slots[block]]
                rows = jnp.dot(place, window, preferred_element_type=F32).astype(BF16)
                dense_buf[slot, low : low + caps[block], half * 128 : (half + 1) * 128] = rows
            accumulate(block, group, dense_buf[slot, low : low + caps[block], :])
        dense_out(group, slot).start()

    def table(block):
        return meta_refs[0] if block == 0 else got_refs[block - 1]

    def owners(block):
        ids = table(block)[tiles + hours : tiles + hours + 8, :].astype(F32)[:1]
        rows = lax.broadcasted_iota(jnp.int32, (obs, caps[block]), 0).astype(F32) + 1.0
        return (rows == ids).astype(F32).astype(BF16)

    def partial_of(block):
        match = table(block)[tiles : tiles + hours, :].astype(F32)
        found = found_refs[block][...].reshape(samples, hours, caps[block])
        return split_dot(jnp.sum(found * match[None], axis=1), owners(block), 1, 1)

    def step_through(index, carry):
        @pl.when(index < groups)
        def _():
            pack(index)

        @pl.when(index == groups)
        def _():
            launch(groups - 1)
            total_buf[...] = partial_of(0)
            match_refs[0][...] = table(0)[tiles : tiles + hours, :]

        @pl.when((index >= RELAY_LAG) & (index < groups + RELAY_LAG))
        def _():
            relay(index - RELAY_LAG)

        @pl.when(index == UNPACK_LAG)
        def _():
            receive_tables()

        @pl.when(index >= UNPACK_LAG)
        def _():
            unpack(index - UNPACK_LAG)
        return carry

    lax.fori_loop(0, groups + UNPACK_LAG, step_through, 0)
    for group in range(max(0, groups - 2), groups):
        local_out(group, group % 2).wait()
    for group in range(max(0, groups - 2), groups):
        dense_out(group, group % 2).wait()
    flag_out[...] = flag_buf[len(hops) + 1][:1, :1]

    def part_copy(block, target):
        return remote(part_own.at[block - 1], part_in.at[block - 1], part_send.at[block - 1], part_recv.at[block - 1], to(target))

    def part_start(block):
        @pl.when(me + block < axis)
        def _():
            part_copy(block, me + block).start()

    for block in blocks:
        @pl.when(me < block)
        def _():
            part_in[block - 1] = jnp.zeros((samples, obs), F32)
    for block in reversed(blocks):
        part_own[block - 1] = partial_of(block)
        if block < reach:
            part_start(block + 1)
    for block in blocks:
        match_refs[block][...] = table(block)[tiles : tiles + hours, :]
    part_start(1)
    total = total_buf[...]
    for block in blocks:
        @pl.when(me >= block)
        def _():
            part_copy(block, me).wait_recv()
        total = total + part_in[block - 1]
    total_buf[...] = total
    swap = remote(total_buf, other_buf, core_sem.at[0], core_sem.at[1], {"cells": 1 - core})
    swap.start()
    swap.wait()
    modeled = total_buf[...] + other_buf[...]
    modeled_ref[...] = modeled
    residual = (weight_ref[...] * (modeled - value_ref[...])).astype(BF16)
    res_buf[...] = residual

    def res_copy(block, target):
        return remote(res_buf, res_in.at[block - 1], res_send.at[block - 1], res_recv.at[block - 1], to(target))

    line_refs[0][...] = contract(residual, owners(0), 1, 0).astype(BF16)
    for block in reversed(blocks):
        @pl.when(me >= block)
        def _():
            res_copy(block, me - block).start()

        @pl.when(me + block >= axis)
        def _():
            res_in[block - 1] = jnp.zeros((samples, obs), BF16)
    for block in blocks:
        @pl.when(me + block < axis)
        def _():
            res_copy(block, me).wait_recv()
        line_refs[block][...] = contract(res_in[block - 1], owners(block), 1, 0).astype(BF16)

    for block in blocks:
        @pl.when(me >= block)
        def _():
            meta_copy(block, me).wait_send()
            res_copy(block, me).wait_send()

        @pl.when(me + block < axis)
        def _():
            part_copy(block, me).wait_send()

    def drain(group, carry):
        for block in blocks:
            @pl.when(me >= block)
            def _():
                bulk_copy(block, group, send_refs[block - 1].at[group], me).wait_send()
        if relays:
            @pl.when(is_two & (lax.rem(group, 4) != 2))
            def _():
                forward_two(group).wait_send()

            @pl.when(is_one & (lax.rem(group, 4) == 2))
            def _():
                forward_one(group).wait_send()
        return carry

    lax.fori_loop(0, groups, drain, 0)


def exchange(caps, slots, pairs, flux, footprint, pos, flag, metas, obs_value, obs_weight, axis):
    samples, hours, cells = flux.shape
    obs, bands, _ = footprint.shape
    tiles = pos.shape[0]
    reach = len(caps) - 1
    groups = tiles // GROUP
    wide = GROUP * 128
    lines = samples * hours
    hop_count = max(1, math.ceil(math.log2(axis)))
    vmem = pl.BlockSpec(memory_space=pltpu.VMEM)
    anywhere = pl.BlockSpec(memory_space=pl.ANY)
    dma = pltpu.SemaphoreType.DMA
    depth = sum(caps)
    out_shape = [
        jax.ShapeDtypeStruct((depth, cells), BF16),
        jax.ShapeDtypeStruct((samples, obs), F32),
        jax.ShapeDtypeStruct((1, 1), F32),
    ]
    out_shape += [jax.ShapeDtypeStruct((samples, cap), BF16) for cap in caps]
    out_shape += [jax.ShapeDtypeStruct((hours, cap), BF16) for cap in caps]
    scratch = [
        pltpu.VMEM((2, obs, bands, wide), BF16),
        pltpu.VMEM((lines, cells), BF16),
        pltpu.VMEM((2, caps[0], wide), BF16),
        pltpu.VMEM((2, depth - caps[0], wide), BF16),
        pltpu.VMEM((reach, samples, obs), F32),
        pltpu.VMEM((reach, samples, obs), F32),
        pltpu.VMEM((samples, obs), F32),
        pltpu.VMEM((samples, obs), F32),
        pltpu.VMEM((samples, obs), BF16),
        pltpu.VMEM((reach, samples, obs), BF16),
        pltpu.VMEM((hop_count + 2, 8, 128), F32),
        pltpu.VMEM((hop_count + 1, 8, 128), F32),
    ]
    scratch += [pltpu.VMEM((groups, pair, 128), BF16) for pair in pairs[1:]] * 2
    scratch += [pltpu.VMEM((lines, cap), F32) for cap in caps]
    scratch += [pltpu.VMEM(metas[0].shape[:1] + (cap,), BF16) for cap in caps[1:]]
    scratch += [pltpu.VMEM((cap, 128), BF16) for cap in caps[1:]]
    scratch += [
        pltpu.VMEM((groups, pairs[min(2, reach)], 128), BF16),
        pltpu.VMEM((max(1, groups // 4), pairs[1], 128), BF16),
    ]
    scratch += [
        dma((2,)), dma, dma((2,)), dma((2,)),
        dma((reach, groups)), dma((reach, groups)),
        dma((groups,)), dma((groups,)), dma((max(1, groups // 4),)), dma((max(1, groups // 4),)),
        dma((reach,)), dma((reach,)), dma((reach,)), dma((reach,)),
        dma((2,)), dma((reach,)), dma((reach,)), dma((2, hop_count + 1)),
    ]
    geometry = (caps, slots, pairs, tiles, hours, axis)
    return pl.pallas_call(
        functools.partial(bulk_kernel, geometry),
        in_specs=[anywhere, anywhere] + [vmem] * (4 + len(metas)),
        out_specs=[anywhere] + [vmem] * (len(out_shape) - 1),
        out_shape=out_shape,
        scratch_shapes=scratch,
        compiler_params=pltpu.CompilerParams(
            collective_id=0, has_side_effects=True, vmem_limit_bytes=VMEM_LIMIT),
        name="bulk",
    )(footprint, flux.reshape(lines, cells), pos, flag, obs_value, obs_weight[None, :], *metas)


def adjoint_kernel(count, *refs):
    dense_ref, modeled_ref, out_ref, kept_ref, line_buf = refs[2 * count :]

    @pl.when(pl.program_id(0) == 0)
    def _():
        pieces = []
        for line, match in zip(refs[:count], refs[count : 2 * count]):
            values = line[...].astype(F32)[:, None, :] * match[...].astype(F32)[None]
            pieces.append(values.reshape(-1, values.shape[2]))
        line_buf[...] = jnp.concatenate(pieces, axis=1).astype(BF16)
        kept_ref[...] = modeled_ref[...]

    out_ref[...] = jnp.dot(line_buf[...], dense_ref[...], preferred_element_type=F32)


def adjoint(lines, matches, dense, modeled):
    depth, cells = dense.shape
    tile = min(TILE_CELLS, cells)
    height = lines[0].shape[0] * matches[0].shape[0]
    whole = [pl.BlockSpec(part.shape, lambda i: (0, 0)) for part in lines + matches]
    return pl.pallas_call(
        functools.partial(adjoint_kernel, len(lines)),
        grid=(cells // tile,),
        in_specs=whole + [pl.BlockSpec((depth, tile), lambda i: (0, i)), pl.BlockSpec(modeled.shape, lambda i: (0, 0))],
        out_specs=[pl.BlockSpec((height, tile), lambda i: (0, i)), pl.BlockSpec(modeled.shape, lambda i: (0, 0))],
        out_shape=[
            jax.ShapeDtypeStruct((height, cells), F32),
            jax.ShapeDtypeStruct(modeled.shape, F32),
        ],
        scratch_shapes=[pltpu.VMEM((height, depth), BF16)],
        compiler_params=pltpu.CompilerParams(
            dimension_semantics=("arbitrary",), vmem_limit_bytes=VMEM_LIMIT),
        name="adjoint",
    )(*lines, *matches, dense, modeled)


def whole_plan(reach, flux, footprint, band_lag, obs_hour, tile_mask, obs_value, obs_weight):
    samples, hours, cells = flux.shape
    obs, bands, _ = footprint.shape
    rows = obs * bands
    position = lax.axis_index("tm")
    tiles = tile_mask.shape[1]
    source = (obs_hour[:, None] - band_lag).reshape(1, rows)
    hour_ids = lax.broadcasted_iota(jnp.int32, (hours, rows), 0)
    obs_ids = lax.broadcasted_iota(jnp.int32, (rows, obs), 0) // bands
    owner = (obs_ids == lax.broadcasted_iota(jnp.int32, (rows, obs), 1)).astype(BF16)
    masked = footprint.reshape(obs, bands, tiles, cells // tiles) * tile_mask.astype(BF16)[:, None, :, None]
    masked = masked.reshape(rows, cells)
    flux_lines = flux.reshape(samples * hours, cells)
    blocks = range(reach + 1)

    def sent(value, steps):
        return shifted(value, "tm", steps) if steps else value

    prints, matches = [], []
    for block in blocks:
        match = ((source == hour_ids + (position - block) * hours) & (source >= 0)).astype(BF16)
        prints.append(sent(masked, -block))
        matches.append(sent(match, -block))
    prints, matches = jnp.stack(prints), jnp.stack(matches)

    def forward(pair):
        found = contract(flux_lines, pair[0], 1, 1).reshape(samples, hours, rows)
        return jnp.sum(found * pair[1].astype(F32)[None], axis=1)

    found = lax.map(forward, (prints, matches))
    total = sum(sent(found[block], block) for block in blocks)
    total = contract(total, owner.astype(F32), 1, 0, precision=lax.Precision.HIGHEST)
    modeled = over_axis(total, "cells")
    residual = (obs_weight[None, :] * (modeled - obs_value)).astype(BF16)
    values = contract(residual, owner, 1, 1, BF16)
    values = jnp.stack([sent(values, -block) for block in blocks])

    def backward(gradient, parts):
        lines = (parts[0][:, None, :] * parts[1][None]).reshape(samples * hours, rows)
        return gradient + contract(lines, parts[2], 1, 0), None

    gradient = jnp.zeros((samples * hours, cells), F32)
    gradient, _ = lax.scan(backward, gradient, (values, matches, prints))
    return modeled, gradient


def body(axis, flux, footprint, band_lag, obs_hour, tile_mask, obs_value, obs_weight):
    samples, hours, cells = flux.shape
    obs, bands, _ = footprint.shape
    tiles = tile_mask.shape[1]
    reach = -(-(LAGS - 1) // hours)
    sizes = [capacities(block, hours, obs, bands) for block in range(reach + 1)]
    caps = tuple(size[0] for size in sizes)
    slots = tuple(size[1] for size in sizes)
    pairs = tuple(size[2] for size in sizes)
    pos, flag, *metas = prepare(caps, slots, pairs, hours, band_lag, obs_hour, tile_mask)
    outs = exchange(caps, slots, pairs, flux, footprint, pos, flag, metas, obs_value, obs_weight, axis)
    dense, modeled, flags = outs[:3]
    lines = list(outs[3 : 4 + reach])
    matches = list(outs[4 + reach :])

    def slow():
        return whole_plan(reach, flux, footprint, band_lag, obs_hour, tile_mask, obs_value, obs_weight)

    def fast():
        gradient, kept = adjoint(lines, matches, dense, modeled)
        return kept, gradient

    modeled, gradient = lax.cond(flags[0, 0] > 0, slow, fast)
    return modeled, gradient.reshape(samples, hours, cells)


def solution(mesh):
    placed = (
        P(None, "tm", "cells"),
        P("tm", None, "cells"),
        P("tm", None),
        P("tm"),
        P("tm", "cells"),
        P(None, "tm"),
        P("tm"),
    )
    return jax.shard_map(
        functools.partial(body, mesh.shape["tm"]),
        mesh=mesh,
        in_specs=placed,
        out_specs=(P(None, "tm"), P(None, "tm", "cells")),
        check_vma=False,
    )
```

```python
import functools
import math

import jax
import jax.numpy as jnp
import numpy as np
from jax import lax
from jax.experimental import pallas as pl
from jax.experimental.pallas import tpu as pltpu
from jax.sharding import PartitionSpec as P

LAGS = 24
GRAIN = 16
GROUP = 2
UNPACK_LAG = 4
RELAY_LAG = 3
TILE_CELLS = 1024
VMEM_LIMIT = 62 * 2**20
MESH = pl.DeviceIdType.MESH
BF16 = jnp.bfloat16
F32 = jnp.float32


def shifted(value, axis, steps):
    count = lax.axis_size(axis)
    initial, last = (max(0, -steps), min(count, count - steps))
    return lax.ppermute(value, axis, [(source, source + steps) for source in range(initial, last)])


def over_axis(value, axis):
    if lax.axis_size(axis) == 2:
        return value + lax.ppermute(value, axis, [(0, 1), (1, 0)])
    return lax.psum(value, axis)


def contract(left, right, left_dim, right_dim, out=F32, precision=None):
    return lax.dot_general(
        left, right, (((left_dim,), (right_dim,)), ((), ())),
        precision=precision, preferred_element_type=out,
    )


def capacities(block, hours, obs, bands):
    mean = spread = mean_square = 0.0
    for hour in range(hours):
        hits = sum(1 for lag in range(LAGS) if (hour - lag) // hours == -block)
        share = hits / LAGS
        mean += bands * share / hours
        mean_square += (bands * share) ** 2 / hours
        spread += bands * share * (1 - share) * (LAGS - bands) / (LAGS - 1) / hours
    spread += mean_square - mean**2
    rows = obs * mean + 4.0 * math.sqrt(obs * spread)
    half_spread = 0.5 * (spread + mean**2) - 0.25 * mean**2
    slots = 0.5 * obs * mean + 4.7 * math.sqrt(obs * half_spread)
    pair_spread = 1.5 * (spread + mean**2) - mean**2
    pairs = obs * mean + 4.65 * math.sqrt(obs * pair_spread)
    rows = min(obs * bands, GRAIN * math.ceil(rows / GRAIN))
    slots = min(rows, GRAIN * math.ceil(slots / GRAIN))
    return rows, slots, max(slots, min(2 * slots, GRAIN * math.ceil(pairs / GRAIN)))


def prep_kernel(caps, slots, pairs, lag_ref, hour_ref, mask_ref, band_ref, pos_ref, flag_ref, *meta_refs):
    reach = len(caps) - 1
    bands, obs = lag_ref.shape
    tiles = mask_ref.shape[0]
    rows = bands * obs
    hours = meta_refs[0].shape[0] - tiles - 8
    position = lax.axis_index("tm")
    first = (position - reach) * hours
    row_ids = lax.broadcasted_iota(jnp.int32, (obs, rows), 1)
    obs_ids = lax.broadcasted_iota(jnp.int32, (obs, rows), 0)
    spread = ((row_ids >= obs_ids * bands) & (row_ids < (obs_ids + 1) * bands)).astype(F32).astype(BF16)
    ahead = hour_ref[...] - lag_ref[...] - first
    ahead = jnp.concatenate([ahead, jnp.zeros((8 - bands % 8, obs), jnp.int32)], axis=0) if bands % 8 else ahead
    ahead = jnp.dot(ahead.astype(F32).astype(BF16), spread, preferred_element_type=F32)
    ahead = jnp.sum(ahead * band_ref[...], axis=0, keepdims=True)
    on = jnp.dot(mask_ref[...].astype(F32).astype(BF16), spread, preferred_element_type=F32)
    ids = lax.broadcasted_iota(jnp.int32, (8, obs), 1).astype(F32) + 1.0
    ids = jnp.dot(ids.astype(BF16), spread, preferred_element_type=F32)[:1]
    valid = ahead >= (-first).astype(F32)
    members, lines = [], []
    for block in range(reach + 1):
        low = hours * (reach - block)
        member = (ahead >= low) & (ahead < low + hours) & valid
        members.append(member.astype(F32))
    head = jnp.concatenate(members + [jnp.zeros((8 - (reach + 1) % 8, rows), F32)], axis=0)
    lines = [head] + [members[block] * on for block in range(1, reach + 1)]
    before = lax.broadcasted_iota(jnp.int32, (rows, rows), 0) < lax.broadcasted_iota(jnp.int32, (rows, rows), 1)
    before = before.astype(F32).astype(BF16)
    ranks = jnp.dot(jnp.concatenate(lines, axis=0).astype(BF16), before, preferred_element_type=F32)
    over = jnp.zeros((1, rows), F32)
    pos = jnp.full((tiles, rows), -1.0, F32)
    tile_ids = lax.broadcasted_iota(jnp.int32, (tiles, rows), 0)
    odd = (tile_ids & 1) == 1
    halves = lax.broadcasted_iota(jnp.int32, (tiles, tiles), 0) >> 1
    halves = (halves == (lax.broadcasted_iota(jnp.int32, (tiles, tiles), 1) >> 1)).astype(F32).astype(BF16)
    crowded = jnp.zeros((tiles, 1), F32)
    base = caps[0]
    for block in range(reach + 1):
        member = members[block]
        rank = ranks[block : block + 1]
        over = jnp.maximum(over, jnp.where((member > 0) & (rank >= caps[block]), 1.0, 0.0))
        row_slot = jnp.where(member > 0, rank, -1.0)
        if block == 0:
            pos = jnp.where((member * on > 0) & (rank < caps[0]), rank, pos)
            order = jnp.zeros((tiles, rows), F32)
        else:
            start = head.shape[0] + (block - 1) * tiles
            tile_rank = ranks[start : start + tiles]
            inside = member * on > 0
            excess = jnp.where(inside & (tile_rank >= slots[block]), 1.0, 0.0)
            over = jnp.maximum(over, jnp.max(excess, axis=0, keepdims=True))
            both = jnp.dot(halves, inside.astype(F32).astype(BF16), preferred_element_type=F32)
            both = jnp.sum(both, axis=1, keepdims=True)
            crowded = jnp.maximum(crowded, jnp.where(both > pairs[block], 1.0, 0.0))
            place = jnp.where(odd, slots[block] - 1.0 - tile_rank, tile_rank)
            pos = jnp.where(inside & (tile_rank < slots[block]), place + base, pos)
            order = jnp.where(inside, place + 1.0, 0.0)
            base += slots[block]
        hour_of = lax.broadcasted_iota(jnp.int32, (hours, rows), 0).astype(F32) + float(hours * (reach - block))
        match = jnp.where((ahead == hour_of) & valid, 1.0, 0.0)
        tail = jnp.where(lax.broadcasted_iota(jnp.int32, (8, rows), 0) == 0, ids, 0.0)
        values = jnp.concatenate([order, match, tail], axis=0).astype(BF16)
        select = lax.broadcasted_iota(jnp.int32, (caps[block], rows), 0).astype(F32) == row_slot
        select = select.astype(F32).astype(BF16)
        meta_refs[block][...] = contract(values, select, 1, 1).astype(BF16)
    pos_ref[...] = pos
    over = jnp.maximum(jnp.max(over, axis=1, keepdims=True), jnp.max(crowded, axis=0, keepdims=True))
    flag_ref[...] = jnp.broadcast_to(over, (8, 128))


def prepare(caps, slots, pairs, hours, band_lag, obs_hour, tile_mask):
    obs, bands = band_lag.shape
    tiles = tile_mask.shape[1]
    rows = obs * bands
    pad = bands + (8 - bands % 8 if bands % 8 else 0)
    band = np.equal(np.arange(rows) % bands, np.arange(pad)[:, None]).astype(np.float32)
    vmem = pl.BlockSpec(memory_space=pltpu.VMEM)
    shapes = [
        jax.ShapeDtypeStruct((tiles, rows), F32),
        jax.ShapeDtypeStruct((8, 128), F32),
    ] + [jax.ShapeDtypeStruct((tiles + hours + 8, cap), BF16) for cap in caps]
    return pl.pallas_call(
        functools.partial(prep_kernel, caps, slots, pairs),
        in_specs=[vmem] * 4,
        out_specs=[vmem] * len(shapes),
        out_shape=shapes,
        compiler_params=pltpu.CompilerParams(vmem_limit_bytes=VMEM_LIMIT),
        name="prep",
    )(band_lag.T, obs_hour[None, :], tile_mask.T, band)


def split_dot(left, right, left_dim, right_dim):
    total = None
    for _ in range(3):
        term = left.astype(BF16)
        left = left - term.astype(F32)
        part = contract(term, right, left_dim, right_dim)
        total = part if total is None else total + part
    return total


def bulk_kernel(geometry, *refs):
    caps, slots, pairs, tiles, hours, axis = geometry
    reach = len(caps) - 1
    blocks = range(1, reach + 1)
    refs = list(refs)

    def take(count):
        head = refs[:count]
        del refs[:count]
        return head

    (prints_ref, flux_hbm, pos_ref, flag_ref, value_ref, weight_ref) = take(6)
    meta_refs = take(reach + 1)
    (dense_ref, modeled_ref, flag_out) = take(3)
    line_refs = take(reach + 1)
    match_refs = take(reach + 1)
    (prints_buf, flux_ref, local_buf, dense_buf, part_own, part_in, total_buf, other_buf,
     res_buf, res_in, flag_buf, flag_in) = take(12)
    send_refs, recv_refs, found_refs, got_refs, column_refs = (
        take(reach), take(reach), take(reach + 1), take(reach), take(reach))
    (relay_ref, relay_one) = take(2)
    (prints_sem, flux_sem, local_sem, dense_sem, send_sem, recv_sem, relay_in_sem, relay_out_sem,
     one_in_sem, one_out_sem, meta_send, meta_recv, part_send, part_recv, core_sem, res_send, res_recv,
     flag_sem) = take(18)

    me = lax.axis_index("tm")
    core = lax.axis_index("cells")
    obs = value_ref.shape[1]
    samples = value_ref.shape[0]
    groups = tiles // GROUP
    wide = GROUP * 128
    quad = lax.rem(me, 4)
    relays = axis % 4 == 0 and reach >= 2

    def to(tm):
        return {"tm": tm}

    partners = [step for step in (1, 2, 3, 4) if step < axis]
    hops = []
    step = 1
    while step < axis:
        hops.append(step)
        step *= 2
    far = [hop for hop in hops if hop > 4]

    def flip(hop):
        return jnp.where(lax.rem(me // hop, 2) == 0, me + hop, me - hop)

    barrier = pltpu.get_barrier_semaphore()
    count = jnp.int32(0)
    for step in partners:
        for target, exists in ((me + step, me + step < axis), (me - step, me >= step)):
            @pl.when(exists)
            def _():
                pl.semaphore_signal(barrier, inc=1, device_id=to(target), device_id_type=MESH)
            count = count + exists.astype(jnp.int32)
    for hop in far:
        pl.semaphore_signal(barrier, inc=1, device_id=to(flip(hop)), device_id_type=MESH)
        count = count + 1
    pl.semaphore_signal(barrier, inc=1, device_id={"cells": 1 - core}, device_id_type=MESH)
    count = count + 1

    def fetch(group, slot):
        return pltpu.make_async_copy(
            prints_ref.at[:, :, pl.ds(pl.multiple_of(group * wide, wide), wide)],
            prints_buf.at[slot], prints_sem.at[slot])

    fetch(0, 0).start()
    flux_copy = pltpu.make_async_copy(flux_hbm, flux_ref, flux_sem)
    flux_copy.start()
    pl.semaphore_wait(barrier, count)

    def remote(src, dst, ssem, rsem, target):
        return pltpu.make_async_remote_copy(
            src_ref=src, dst_ref=dst, send_sem=ssem, recv_sem=rsem,
            device_id=target, device_id_type=MESH)

    def meta_copy(block, target):
        return remote(meta_refs[block], got_refs[block - 1], meta_send.at[block - 1], meta_recv.at[block - 1], to(target))

    for block in blocks:
        @pl.when(me >= block)
        def _():
            meta_copy(block, me - block).start()

    def bulk_copy(block, group, source, target, dst=None, ssem=None, rsem=None):
        return remote(source, recv_refs[block - 1].at[group] if dst is None else dst,
                      send_sem.at[block - 1, group] if ssem is None else ssem,
                      recv_sem.at[block - 1, group] if rsem is None else rsem, to(target))

    def send(block, group):
        source = send_refs[block - 1].at[group]
        exists = me >= block
        detour = None
        if relays and block == 2:
            detour = (quad == 0) & (lax.rem(group, 4) != 2)
            copy = bulk_copy(2, group, source, me + 2, relay_ref.at[group], None, relay_in_sem.at[group])
        elif relays and block == 1:
            detour = (lax.rem(me, 2) == 0) & (lax.rem(group, 4) == 2)
            copy = bulk_copy(1, group, source, jnp.where(quad == 0, me + 2, me - 2),
                             relay_one.at[group // 4], None, one_in_sem.at[group // 4])
        if detour is None:
            @pl.when(exists)
            def _():
                bulk_copy(block, group, source, me - block).start()
        else:
            @pl.when(exists & detour)
            def _():
                copy.start()

            @pl.when(exists & jnp.logical_not(detour))
            def _():
                bulk_copy(block, group, source, me - block).start()

    def forward_two(group):
        return bulk_copy(2, group, relay_ref.at[group], me - 4, None, relay_out_sem.at[group])

    def forward_one(group):
        return bulk_copy(1, group, relay_one.at[group // 4], jnp.where(quad == 0, me + 1, me - 3),
                         None, one_out_sem.at[group // 4])

    is_two = (quad == 2) & (me >= 6)
    is_one = (lax.rem(me, 2) == 0) & (me != 2)
    def relay(group):
        if relays:
            @pl.when(is_two & (lax.rem(group, 4) != 2))
            def _():
                bulk_copy(2, group, send_refs[1].at[group], me - 4, relay_ref.at[group],
                          None, relay_in_sem.at[group]).wait_recv()
                forward_two(group).start()

            @pl.when(is_one & (lax.rem(group, 4) == 2))
            def _():
                bulk_copy(1, group, send_refs[0].at[group], me, relay_one.at[group // 4],
                          None, one_in_sem.at[group // 4]).wait_recv()
                forward_one(group).start()

    def launch(group):
        for block in [2, 1] + list(blocks)[2:] if reach >= 2 else blocks:
            send(block, group)

    for block in blocks:
        @pl.when(me + block >= axis)
        def _():
            recv_refs[block - 1][...] = jnp.zeros_like(recv_refs[block - 1])
            got_refs[block - 1][...] = jnp.zeros_like(got_refs[block - 1])
    flag_buf[0] = flag_ref[...]
    for found in found_refs:
        found[...] = jnp.zeros_like(found)
    flux_copy.wait()

    total_slots = caps[0] + sum(slots[1:])
    starts = [0, caps[0]]
    for block in blocks:
        starts.append(starts[-1] + slots[block])
    bases = [sum(caps[:block]) for block in range(reach + 1)]

    def columns(group):
        return pl.ds(pl.multiple_of(group * wide, wide), wide)

    def local_out(group, slot):
        return pltpu.make_async_copy(local_buf.at[slot], dense_ref.at[pl.ds(0, caps[0]), columns(group)], local_sem.at[slot])

    def dense_out(group, slot):
        return pltpu.make_async_copy(
            dense_buf.at[slot], dense_ref.at[pl.ds(caps[0], sum(caps[1:])), columns(group)], dense_sem.at[slot])

    def accumulate(block, group, rows):
        found_refs[block][...] += contract(flux_ref[:, columns(group)], rows, 1, 1)

    def pack(group):
        slot = lax.rem(group, 2)

        @pl.when(group >= 1)
        def _():
            launch(group - 1)

        fetch(group, slot).wait()

        @pl.when(group + 1 < groups)
        def _():
            fetch(group + 1, 1 - slot).start()

        @pl.when(group >= 2)
        def _():
            local_out(group - 2, slot).wait()

        prints = prints_buf[slot].reshape(prints_buf.shape[1] * prints_buf.shape[2], wide)
        slot_ids = lax.broadcasted_iota(jnp.int32, (total_slots, 1), 0).astype(F32)
        ends = []
        for half in range(GROUP):
            tile = group * GROUP + half
            select = (slot_ids == pos_ref[pl.ds(tile, 1), :]).astype(F32).astype(BF16)
            packed = jnp.dot(select, prints[:, half * 128 : (half + 1) * 128], preferred_element_type=F32).astype(BF16)
            local_buf[slot, :, half * 128 : (half + 1) * 128] = packed[: caps[0]]
            ends.append(packed)
        for block in blocks:
            first, last = (packed[starts[block] : starts[block + 1]] for packed in ends)
            gap, window = pairs[block] - slots[block], slots[block]
            send_refs[block - 1][group, :gap] = first[:gap]
            if window > gap:
                send_refs[block - 1][group, gap:window] = first[gap:] + last[: window - gap]
            send_refs[block - 1][group, window:] = last[window - gap :]
        local_out(group, slot).start()
        accumulate(0, group, local_buf[slot])

    def receive_tables():
        for block in blocks:
            @pl.when(me + block < axis)
            def _():
                meta_copy(block, me).wait_recv()
            meta = got_refs[block - 1][...].astype(F32)
            top = meta[:tiles]
            top = jnp.concatenate([top, jnp.zeros((128 - tiles, top.shape[1]), F32)], axis=0)
            column_refs[block - 1][...] = top.T.astype(BF16)


    def unpack(group):
        slot = lax.rem(group, 2)

        def flag_copy(index):
            target = {"cells": 1 - core} if index == len(hops) else to(flip(hops[index]))
            return remote(flag_buf.at[index], flag_in.at[index], flag_sem.at[0, index], flag_sem.at[1, index], target)

        for index in range(len(hops) + 1):
            @pl.when(group == 2 * index)
            def _():
                flag_copy(index).start()

            @pl.when(group == 2 * index + 1)
            def _():
                flag_copy(index).wait()
                merged = jnp.maximum(flag_buf[index], flag_in[index])
                flag_buf[index + 1] = merged

        @pl.when(group >= 2)
        def _():
            dense_out(group - 2, slot).wait()

        for block in blocks:
            @pl.when(me + block < axis)
            def _():
                bulk_copy(block, group, send_refs[block - 1].at[group], me).wait_recv()
            low = bases[block] - caps[0]
            for half in range(GROUP):
                tile = group * GROUP + half
                pick = lax.broadcasted_iota(jnp.int32, (128, slots[block]), 0) == tile
                spread = jnp.dot(column_refs[block - 1][...], pick.astype(F32).astype(BF16), preferred_element_type=F32)
                ids = lax.broadcasted_iota(jnp.int32, (1, slots[block]), 1).astype(F32) + 1.0
                place = (spread == ids).astype(F32).astype(BF16)
                start = half * (pairs[block] - slots[block])
                window = recv_refs[block - 1][group, start : start + slots[block]]
                rows = jnp.dot(place, window, preferred_element_type=F32).astype(BF16)
                dense_buf[slot, low : low + caps[block], half * 128 : (half + 1) * 128] = rows
            accumulate(block, group, dense_buf[slot, low : low + caps[block], :])
        dense_out(group, slot).start()

    def table(block):
        return meta_refs[0] if block == 0 else got_refs[block - 1]

    def owners(block):
        ids = table(block)[tiles + hours : tiles + hours + 8, :].astype(F32)[:1]
        rows = lax.broadcasted_iota(jnp.int32, (obs, caps[block]), 0).astype(F32) + 1.0
        return (rows == ids).astype(F32).astype(BF16)

    def partial_of(block):
        match = table(block)[tiles : tiles + hours, :].astype(F32)
        found = found_refs[block][...].reshape(samples, hours, caps[block])
        return split_dot(jnp.sum(found * match[None], axis=1), owners(block), 1, 1)

    def step_through(index, carry):
        @pl.when(index < groups)
        def _():
            pack(index)

        @pl.when(index == groups)
        def _():
            launch(groups - 1)
            total_buf[...] = partial_of(0)
            match_refs[0][...] = table(0)[tiles : tiles + hours, :]

        @pl.when((index >= RELAY_LAG) & (index < groups + RELAY_LAG))
        def _():
            relay(index - RELAY_LAG)

        @pl.when(index == UNPACK_LAG)
        def _():
            receive_tables()

        @pl.when(index >= UNPACK_LAG)
        def _():
            unpack(index - UNPACK_LAG)
        return carry

    lax.fori_loop(0, groups + UNPACK_LAG, step_through, 0)
    for group in range(max(0, groups - 2), groups):
        local_out(group, group % 2).wait()
    for group in range(max(0, groups - 2), groups):
        dense_out(group, group % 2).wait()
    flag_out[...] = flag_buf[len(hops) + 1][:1, :1]

    def part_copy(block, target):
        return remote(part_own.at[block - 1], part_in.at[block - 1], part_send.at[block - 1], part_recv.at[block - 1], to(target))

    def part_start(block):
        @pl.when(me + block < axis)
        def _():
            part_copy(block, me + block).start()

    for block in blocks:
        @pl.when(me < block)
        def _():
            part_in[block - 1] = jnp.zeros((samples, obs), F32)
    for block in reversed(blocks):
        part_own[block - 1] = partial_of(block)
        if block < reach:
            part_start(block + 1)
    for block in blocks:
        match_refs[block][...] = table(block)[tiles : tiles + hours, :]
    part_start(1)
    total = total_buf[...]
    for block in blocks:
        @pl.when(me >= block)
        def _():
            part_copy(block, me).wait_recv()
        total = total + part_in[block - 1]
    total_buf[...] = total
    swap = remote(total_buf, other_buf, core_sem.at[0], core_sem.at[1], {"cells": 1 - core})
    swap.start()
    swap.wait()
    modeled = total_buf[...] + other_buf[...]
    modeled_ref[...] = modeled
    residual = (weight_ref[...] * (modeled - value_ref[...])).astype(BF16)
    res_buf[...] = residual

    def res_copy(block, target):
        return remote(res_buf, res_in.at[block - 1], res_send.at[block - 1], res_recv.at[block - 1], to(target))

    line_refs[0][...] = contract(residual, owners(0), 1, 0).astype(BF16)
    for block in reversed(blocks):
        @pl.when(me >= block)
        def _():
            res_copy(block, me - block).start()

        @pl.when(me + block >= axis)
        def _():
            res_in[block - 1] = jnp.zeros((samples, obs), BF16)
    for block in blocks:
        @pl.when(me + block < axis)
        def _():
            res_copy(block, me).wait_recv()
        line_refs[block][...] = contract(res_in[block - 1], owners(block), 1, 0).astype(BF16)

    for block in blocks:
        @pl.when(me >= block)
        def _():
            meta_copy(block, me).wait_send()
            res_copy(block, me).wait_send()

        @pl.when(me + block < axis)
        def _():
            part_copy(block, me).wait_send()

    def drain(group, carry):
        for block in blocks:
            @pl.when(me >= block)
            def _():
                bulk_copy(block, group, send_refs[block - 1].at[group], me).wait_send()
        if relays:
            @pl.when(is_two & (lax.rem(group, 4) != 2))
            def _():
                forward_two(group).wait_send()

            @pl.when(is_one & (lax.rem(group, 4) == 2))
            def _():
                forward_one(group).wait_send()
        return carry

    lax.fori_loop(0, groups, drain, 0)


def exchange(caps, slots, pairs, flux, footprint, pos, flag, metas, obs_value, obs_weight, axis):
    samples, hours, cells = flux.shape
    obs, bands, _ = footprint.shape
    tiles = pos.shape[0]
    reach = len(caps) - 1
    groups = tiles // GROUP
    wide = GROUP * 128
    lines = samples * hours
    hop_count = max(1, math.ceil(math.log2(axis)))
    vmem = pl.BlockSpec(memory_space=pltpu.VMEM)
    anywhere = pl.BlockSpec(memory_space=pl.ANY)
    dma = pltpu.SemaphoreType.DMA
    depth = sum(caps)
    out_shape = [
        jax.ShapeDtypeStruct((depth, cells), BF16),
        jax.ShapeDtypeStruct((samples, obs), F32),
        jax.ShapeDtypeStruct((1, 1), F32),
    ]
    out_shape += [jax.ShapeDtypeStruct((samples, cap), BF16) for cap in caps]
    out_shape += [jax.ShapeDtypeStruct((hours, cap), BF16) for cap in caps]
    scratch = [
        pltpu.VMEM((2, obs, bands, wide), BF16),
        pltpu.VMEM((lines, cells), BF16),
        pltpu.VMEM((2, caps[0], wide), BF16),
        pltpu.VMEM((2, depth - caps[0], wide), BF16),
        pltpu.VMEM((reach, samples, obs), F32),
        pltpu.VMEM((reach, samples, obs), F32),
        pltpu.VMEM((samples, obs), F32),
        pltpu.VMEM((samples, obs), F32),
        pltpu.VMEM((samples, obs), BF16),
        pltpu.VMEM((reach, samples, obs), BF16),
        pltpu.VMEM((hop_count + 2, 8, 128), F32),
        pltpu.VMEM((hop_count + 1, 8, 128), F32),
    ]
    scratch += [pltpu.VMEM((groups, pair, 128), BF16) for pair in pairs[1:]] * 2
    scratch += [pltpu.VMEM((lines, cap), F32) for cap in caps]
    scratch += [pltpu.VMEM(metas[0].shape[:1] + (cap,), BF16) for cap in caps[1:]]
    scratch += [pltpu.VMEM((cap, 128), BF16) for cap in caps[1:]]
    scratch += [
        pltpu.VMEM((groups, pairs[min(2, reach)], 128), BF16),
        pltpu.VMEM((max(1, groups // 4), pairs[1], 128), BF16),
    ]
    scratch += [
        dma((2,)), dma, dma((2,)), dma((2,)),
        dma((reach, groups)), dma((reach, groups)),
        dma((groups,)), dma((groups,)), dma((max(1, groups // 4),)), dma((max(1, groups // 4),)),
        dma((reach,)), dma((reach,)), dma((reach,)), dma((reach,)),
        dma((2,)), dma((reach,)), dma((reach,)), dma((2, hop_count + 1)),
    ]
    geometry = (caps, slots, pairs, tiles, hours, axis)
    return pl.pallas_call(
        functools.partial(bulk_kernel, geometry),
        in_specs=[anywhere, anywhere] + [vmem] * (4 + len(metas)),
        out_specs=[anywhere] + [vmem] * (len(out_shape) - 1),
        out_shape=out_shape,
        scratch_shapes=scratch,
        compiler_params=pltpu.CompilerParams(
            collective_id=0, has_side_effects=True, vmem_limit_bytes=VMEM_LIMIT),
        name="bulk",
    )(footprint, flux.reshape(lines, cells), pos, flag, obs_value, obs_weight[None, :], *metas)


def adjoint_kernel(count, *refs):
    dense_ref, modeled_ref, out_ref, kept_ref, line_buf = refs[2 * count :]

    @pl.when(pl.program_id(0) == 0)
    def _():
        pieces = []
        for line, match in zip(refs[:count], refs[count : 2 * count]):
            values = line[...].astype(F32)[:, None, :] * match[...].astype(F32)[None]
            pieces.append(values.reshape(-1, values.shape[2]))
        line_buf[...] = jnp.concatenate(pieces, axis=1).astype(BF16)
        kept_ref[...] = modeled_ref[...]

    out_ref[...] = jnp.dot(line_buf[...], dense_ref[...], preferred_element_type=F32)


def adjoint(lines, matches, dense, modeled):
    depth, cells = dense.shape
    tile = min(TILE_CELLS, cells)
    height = lines[0].shape[0] * matches[0].shape[0]
    whole = [pl.BlockSpec(part.shape, lambda i: (0, 0)) for part in lines + matches]
    return pl.pallas_call(
        functools.partial(adjoint_kernel, len(lines)),
        grid=(cells // tile,),
        in_specs=whole + [pl.BlockSpec((depth, tile), lambda i: (0, i)), pl.BlockSpec(modeled.shape, lambda i: (0, 0))],
        out_specs=[pl.BlockSpec((height, tile), lambda i: (0, i)), pl.BlockSpec(modeled.shape, lambda i: (0, 0))],
        out_shape=[
            jax.ShapeDtypeStruct((height, cells), F32),
            jax.ShapeDtypeStruct(modeled.shape, F32),
        ],
        scratch_shapes=[pltpu.VMEM((height, depth), BF16)],
        compiler_params=pltpu.CompilerParams(
            dimension_semantics=("arbitrary",), vmem_limit_bytes=VMEM_LIMIT),
        name="adjoint",
    )(*lines, *matches, dense, modeled)


def whole_plan(reach, flux, footprint, band_lag, obs_hour, tile_mask, obs_value, obs_weight):
    samples, hours, cells = flux.shape
    obs, bands, _ = footprint.shape
    rows = obs * bands
    position = lax.axis_index("tm")
    tiles = tile_mask.shape[1]
    source = (obs_hour[:, None] - band_lag).reshape(1, rows)
    hour_ids = lax.broadcasted_iota(jnp.int32, (hours, rows), 0)
    obs_ids = lax.broadcasted_iota(jnp.int32, (rows, obs), 0) // bands
    owner = (obs_ids == lax.broadcasted_iota(jnp.int32, (rows, obs), 1)).astype(BF16)
    masked = footprint.reshape(obs, bands, tiles, cells // tiles) * tile_mask.astype(BF16)[:, None, :, None]
    masked = masked.reshape(rows, cells)
    flux_lines = flux.reshape(samples * hours, cells)
    blocks = range(reach + 1)

    def sent(value, steps):
        return shifted(value, "tm", steps) if steps else value

    prints, matches = [], []
    for block in blocks:
        match = ((source == hour_ids + (position - block) * hours) & (source >= 0)).astype(BF16)
        prints.append(sent(masked, -block))
        matches.append(sent(match, -block))
    prints, matches = jnp.stack(prints), jnp.stack(matches)

    def forward(pair):
        found = contract(flux_lines, pair[0], 1, 1).reshape(samples, hours, rows)
        return jnp.sum(found * pair[1].astype(F32)[None], axis=1)

    found = lax.map(forward, (prints, matches))
    total = sum(sent(found[block], block) for block in blocks)
    total = contract(total, owner.astype(F32), 1, 0, precision=lax.Precision.HIGHEST)
    modeled = over_axis(total, "cells")
    residual = (obs_weight[None, :] * (modeled - obs_value)).astype(BF16)
    values = contract(residual, owner, 1, 1, BF16)
    values = jnp.stack([sent(values, -block) for block in blocks])

    def backward(gradient, parts):
        lines = (parts[0][:, None, :] * parts[1][None]).reshape(samples * hours, rows)
        return gradient + contract(lines, parts[2], 1, 0), None

    gradient = jnp.zeros((samples * hours, cells), F32)
    gradient, _ = lax.scan(backward, gradient, (values, matches, prints))
    return modeled, gradient


def body(axis, flux, footprint, band_lag, obs_hour, tile_mask, obs_value, obs_weight):
    samples, hours, cells = flux.shape
    obs, bands, _ = footprint.shape
    tiles = tile_mask.shape[1]
    reach = -(-(LAGS - 1) // hours)
    sizes = [capacities(block, hours, obs, bands) for block in range(reach + 1)]
    caps = tuple(size[0] for size in sizes)
    slots = tuple(size[1] for size in sizes)
    pairs = tuple(size[2] for size in sizes)
    pos, flag, *metas = prepare(caps, slots, pairs, hours, band_lag, obs_hour, tile_mask)
    outs = exchange(caps, slots, pairs, flux, footprint, pos, flag, metas, obs_value, obs_weight, axis)
    dense, modeled, flags = outs[:3]
    lines = list(outs[3 : 4 + reach])
    matches = list(outs[4 + reach :])

    def slow():
        return whole_plan(reach, flux, footprint, band_lag, obs_hour, tile_mask, obs_value, obs_weight)

    def fast():
        gradient, kept = adjoint(lines, matches, dense, modeled)
        return kept, gradient

    modeled, gradient = lax.cond(flags[0, 0] > 0, slow, fast)
    return modeled, gradient.reshape(samples, hours, cells)


def solution(mesh):
    placed = (
        P(None, "tm", "cells"),
        P("tm", None, "cells"),
        P("tm", None),
        P("tm"),
        P("tm", "cells"),
        P(None, "tm"),
        P("tm"),
    )
    return jax.shard_map(
        functools.partial(body, mesh.shape["tm"]),
        mesh=mesh,
        in_specs=placed,
        out_specs=(P(None, "tm"), P(None, "tm", "cells")),
        check_vma=False,
    )
```
